32 devices in a mesh: seq: 8 (over z, x), head: 4 (over y, core).
Axes of the slice: x: 2, y: 2, z: 4, core: 2. Of those that a mesh axis runs over, the one named last changes fastest.
Arguments:
- queries: bfloat16 [1024, 2048], P('seq', 'head'), may hold values from -200 to 200
- keys: bfloat16 [1024, 2048], P('seq', 'head'), may hold values from -6 to 6
- values: bfloat16 [1024, 2048], P('seq', 'head'), may hold values from -6 to 6
- bucket: int32 [1024, 1], replicated, may hold values from 0 to 7; in each aligned block of 128 rows (0 to 127, 128 to 255, ...) at most 24 rows name the same one
- w_out: bfloat16 [2048, 4096], P('head'), may hold values from -0.125 to 0.125
- grad_out: bfloat16 [1024, 4096], P('seq'), may hold values from -6 to 6
Outputs:
- layer_out: bfloat16 [1024, 4096], P('seq', 'head')
- grad_queries: bfloat16 [1024, 2048], P('seq', 'head')
- grad_keys: bfloat16 [1024, 2048], P('seq', 'head')
- grad_values: bfloat16 [1024, 2048], P('seq', 'head')
- grad_weight: float32 [2048, 4096], P('head', 'seq')
The draws below stay inside these ranges and needn't reach their ends.
Inputs may be any that keep to these rules, and one draw needn't show every extreme that they name: Bucket b belongs to the b-th index of seq; buckets b and b-1 are neighbouring tree leaves. Among the tokens of one block of 128 at most 24 share a bucket, and exactly 24 do in some block.
All inputs are finite; a program needn't handle non-finite values.
Results may differ from the reference program's by a relative error of at most 0.012.
Values may be sent and summed in bfloat16 or wider, within the bound.
A program may use at most 128 MiB of HBM per device.

```python
import math
import jax
import jax.numpy as jnp
import numpy as np
from jax import lax

D = 4096
HEADS = 16
HSZ = 128
TOK_DEV = 128
TOKENS = 1024
HD = 2048
CAP = 24
N_SEQ = 8


def query_key(key):
    base = jax.random.fold_in(key, 7)
    first, second = jax.random.split(base, 2)
    shape = (TOKENS, HD)
    keys_part = jnp.clip(jax.random.normal(first, shape, jnp.float32), -6.0, 6.0)
    queries_part = jnp.clip(jax.random.normal(second, shape, jnp.float32), -6.0, 6.0)
    return (queries_part, keys_part)


def draw_queries(key, part):
    return query_key(key)[0].astype(jnp.bfloat16)


def draw_keys(key, part):
    return query_key(key)[1].astype(jnp.bfloat16)


def raised(result, own_key, source, target, blocks, factor):
    def block_of(dim):
        return (jnp.arange(result.shape[dim]) // (result.shape[dim] // blocks)).reshape((-1,) + (1,) * (result.ndim - 1 - dim))

    first = jax.random.permutation(own_key, blocks)[block_of(target)]
    other_side = (block_of(target) + blocks // 2) % blocks
    return jnp.where((block_of(source) == first) | (block_of(source) == other_side), factor * result, result)


def steps_of(stream_key, shape, pieces, least, high):
    def one(position, shards_of):
        heights = jax.random.uniform(jax.random.fold_in(jax.random.fold_in(stream_key, 6), position), (shards_of,), jnp.float32, least / len(pieces), high / len(pieces))
        return jnp.repeat(jnp.exp(heights), shape[position] // shards_of).reshape((-1,) + (1,) * (len(shape) - position - 1))

    level = one(*pieces[0])
    for cut in pieces[1:]:
        level = level * one(*cut)
    return level


def assign_block(stream_key, own, number, rows, count, top, bound, lean):
    order = jax.random.permutation(stream_key, count)
    heavy_load, ordinary = shares(count, rows * top, bound, lean, True), shares(count, rows * top, bound, lean, False)
    places = jnp.arange(count)

    def named(lengths, turn):
        used = int((lengths > 0).sum())
        fixed = max(1, used // 4)
        passed = fixed + (places - fixed + turn * (used - fixed)) % max(1, count - fixed)
        return jnp.zeros((count,), jnp.int32).at[order[jnp.where(places < fixed, places, passed)]].set(jnp.asarray(lengths, jnp.int32))

    lengths = jnp.where(number % 4 == 0, named(heavy_load, number // 4), named(ordinary, number - number // 4 - 1))
    mixed = jax.random.permutation(jax.random.fold_in(own, 3), count)
    giver, sink = mixed[0:count // 2 * 2:2], mixed[1:count // 2 * 2:2]
    slack = jnp.minimum(lengths[giver] - 1, bound - lengths[sink]) // 2
    slack = jnp.where((giver == order[0]) | (sink == order[0]) | (lengths[sink] == 0), 0, jnp.maximum(slack, 0))
    passed = jax.random.randint(jax.random.fold_in(own, 4), (count // 2,), 0, 1 << 20) % (slack + 1)
    lengths = lengths.at[giver].add(-passed).at[sink].add(passed)
    members = jnp.searchsorted(jnp.cumsum(lengths), jnp.arange(rows * top), side="right").astype(jnp.int32)
    table = members.reshape(top, rows).T
    table = table[jax.random.permutation(jax.random.fold_in(own, 1), rows)]
    turn = jax.random.randint(jax.random.fold_in(own, 2), (rows, 1), 0, top)
    return jnp.take_along_axis(table, (jnp.arange(top)[None, :] + turn) % top, axis=1)


def shares(number_of, total, bound, skew, full):
    weights = [(1 << 20) // math.isqrt(rank ** skew) + 1 for rank in range(1, number_of + 1)]
    largest = bound if full else min(bound, max(-(-total // number_of), total * weights[0] // sum(weights)))
    least = 1 if total - largest >= number_of - 1 else 0
    holding, spare = [largest] + [least] * (number_of - 1), total - largest - least * (number_of - 1)
    while spare > 0:
        movable = [i for i in range(1, number_of) if holding[i] < largest] or [i for i in range(1, number_of) if holding[i] < bound]
        whole, remaining = sum([weights[i] for i in movable]), spare
        for i in movable:
            extra = min(bound - holding[i], max(1, remaining * weights[i] // whole), spare)
            holding[i] = holding[i] + extra
            spare = spare - extra
    return np.array(holding)


def centred(key, shape, deviation, reach, cuts=(), kind=jnp.bfloat16):
    gain = steps_of(key, shape, cuts, -0.22, 0.18) if cuts else 1.0
    entries = jax.random.normal(key, shape, jnp.float32) * deviation * gain
    return jnp.minimum(jnp.maximum(entries, -reach), reach).astype(kind)


def gaussian_with(rng, dims, spread, bound, shards, heavy, held_as=jnp.bfloat16):
    drawn = spread * jax.random.normal(rng, dims, jnp.float32)
    if shards:
        drawn = drawn * steps_of(rng, dims, shards, -0.22, 0.18)
    return jnp.clip(raised(drawn, jax.random.fold_in(rng, 3), *heavy), -bound, bound).astype(held_as)


def setup_inputs(seed: int = 0) -> dict:
    streams_of = jax.random.split(jax.random.key(seed), 7)
    queries = draw_queries(jax.random.fold_in(streams_of[6], 71), 0)
    keys = draw_keys(jax.random.fold_in(streams_of[6], 71), 0)
    values = centred(streams_of[2], (TOKENS, HD), 1.0, 6.0, ((0, 8), (1, 4)))
    bucket_keys = jax.random.split(jax.random.fold_in(streams_of[3], 1), TOKENS // TOK_DEV)
    bucket_turns = jax.random.permutation(jax.random.fold_in(streams_of[3], 3), TOKENS // TOK_DEV)
    bucket = jax.vmap(lambda own, number: assign_block(jax.random.fold_in(streams_of[3], 2), own, number, TOK_DEV, N_SEQ, 1, CAP, 2))(bucket_keys, bucket_turns).reshape((TOKENS, 1))
    w_out = centred(streams_of[4], (HD, D), HD ** -0.5, 0.125, ((0, 4),))
    grad_out = gaussian_with(streams_of[5], (TOKENS, D), 1.0, 6.0, ((0, 8),), (0, 1, 8, 2.0))
    return dict(queries=queries, keys=keys, values=values, bucket=bucket, w_out=w_out, grad_out=grad_out)


def member_table(bucket_grid, owner, slot_count):
    matches = (bucket_grid == owner).astype(jnp.int32)
    ranking = jnp.cumsum(matches, axis=1) - matches
    slot_ids = jnp.arange(slot_count, dtype=jnp.int32)
    placed = matches[:, :, None] * (ranking[:, :, None] == slot_ids[None, None, :]).astype(jnp.int32)
    sources = bucket_grid.shape[0]
    stride = bucket_grid.shape[1]
    offsets = jnp.arange(sources, dtype=jnp.int32)[:, None] * stride + jnp.arange(stride, dtype=jnp.int32)[None, :]
    where_at = lax.optimization_barrier(jnp.sum(placed * offsets[:, :, None], axis=1)).reshape(-1)
    present = lax.optimization_barrier(jnp.sum(placed, axis=1)).reshape(-1)
    return (where_at, present)

def allowed_mask(where_here, alive_here, where_before, alive_before):
    amount = where_here.shape[0]
    asking = alive_here[:, None] > 0
    inside = (where_here[None, :] <= where_here[:, None]) & (alive_here[None, :] > 0) & asking
    inside = inside | (jnp.arange(amount)[:, None] == jnp.arange(amount)[None, :])
    earlier = (where_before[None, :] <= where_here[:, None]) & (alive_before[None, :] > 0) & asking
    return jnp.concatenate([inside, earlier], axis=1)

def softmax_rows(scores, allowed):
    masked = jnp.where(allowed[None], scores, -1e+30)
    largest = lax.optimization_barrier(jnp.max(masked, axis=2, keepdims=True))
    weights = jnp.where(allowed[None], jnp.exp(masked - largest), 0.0)
    return weights / lax.optimization_barrier(jnp.sum(weights, axis=2, keepdims=True))

def reference(queries, keys, values, bucket, w_out, grad_out):
    scaling = 1.0 / math.sqrt(HSZ)
    bucket_grid = bucket[:, 0].reshape(N_SEQ, TOK_DEV)
    grad_heads = jnp.dot(grad_out, w_out.T, preferred_element_type=jnp.float32).astype(jnp.bfloat16)

    def gather_rows(source, where_at, present):
        return jnp.take(source, where_at, axis=0) * present[:, None].astype(source.dtype)

    def split_heads(block):
        return block.astype(jnp.float32).reshape(block.shape[0], HEADS, HSZ)

    def flatten(block):
        return block.reshape(block.shape[0], HEADS * HSZ)

    def bucket_pass(owner):
        where_here, alive_here = member_table(bucket_grid, owner, CAP)
        where_before, alive_before = member_table(bucket_grid, owner - 1, CAP)
        allowed = allowed_mask(where_here, alive_here, where_before, alive_before)
        query_rows = split_heads(gather_rows(queries, where_here, alive_here))
        key_all = split_heads(jnp.concatenate([gather_rows(keys, where_here, alive_here), gather_rows(keys, where_before, alive_before)], axis=0))
        value_all = split_heads(jnp.concatenate([gather_rows(values, where_here, alive_here), gather_rows(values, where_before, alive_before)], axis=0))
        grad_rows = split_heads(gather_rows(grad_heads, where_here, alive_here))
        scores = jnp.einsum('qhd,khd->hqk', query_rows, key_all) * scaling
        probs = softmax_rows(scores, allowed)
        rounded = lax.optimization_barrier(probs.astype(jnp.bfloat16)).astype(jnp.float32)
        attended = jnp.einsum('hqk,khd->qhd', rounded, value_all).astype(jnp.bfloat16)
        centre = lax.optimization_barrier(jnp.sum(attended.astype(jnp.float32) * grad_rows, axis=2))
        dprobs = jnp.einsum('qhd,khd->hqk', grad_rows, value_all)
        dscores = probs * (dprobs - jnp.transpose(centre)[:, :, None])
        dround = lax.optimization_barrier(dscores.astype(jnp.bfloat16)).astype(jnp.float32)
        grad_query = (jnp.einsum('hqk,khd->qhd', dround, key_all) * scaling).astype(jnp.bfloat16)
        grad_key = jnp.einsum('hqk,qhd->khd', dround, query_rows) * scaling
        grad_value = jnp.einsum('hqk,qhd->khd', rounded, grad_rows)
        slot_total = where_here.shape[0]
        return (flatten(attended), flatten(grad_query), flatten(grad_key[:slot_total]), flatten(grad_value[:slot_total]), flatten(grad_key[slot_total:]).astype(jnp.bfloat16), flatten(grad_value[slot_total:]).astype(jnp.bfloat16))
    outcome = lax.map(bucket_pass, jnp.arange(N_SEQ, dtype=jnp.int32))
    attended_all, query_all, key_own, value_own, key_prev, value_prev = outcome
    nothing = jnp.zeros_like(key_prev[:1])
    key_next = jnp.concatenate([key_prev[1:], nothing], axis=0)
    value_next = jnp.concatenate([value_prev[1:], nothing], axis=0)
    key_total = (key_own + key_next.astype(jnp.float32)).astype(jnp.bfloat16)
    value_total = (value_own + value_next.astype(jnp.float32)).astype(jnp.bfloat16)
    owners = jnp.arange(N_SEQ, dtype=jnp.int32)
    onehot = (bucket_grid[:, :, None] == owners[None, None, :]).astype(jnp.int32)
    ranking = lax.optimization_barrier(jnp.sum((jnp.cumsum(onehot, axis=1) - onehot) * onehot, axis=2))
    sources = jnp.arange(N_SEQ, dtype=jnp.int32)[:, None]
    lookup = (bucket_grid * (N_SEQ * CAP) + sources * CAP + ranking).reshape(-1).astype(jnp.int32)

    def collect(stacked):
        return jnp.take(stacked.reshape(-1, HEADS * HSZ), lookup, axis=0)
    attended_tok = collect(attended_all)
    layer_out = jnp.dot(attended_tok, w_out, preferred_element_type=jnp.float32).astype(jnp.bfloat16)
    grad_weight = jnp.dot(attended_tok.T, grad_out, preferred_element_type=jnp.float32)
    return (layer_out, collect(query_all), collect(key_total), collect(value_total), grad_weight)
```

```python
import functools
import math

import jax
import jax.numpy as jnp
from jax import lax
from jax.experimental import pallas as pl
from jax.experimental.pallas import tpu as pltpu
from jax.sharding import PartitionSpec as P

HSZ = 128


def passed_along(value, axis, by):
    length = lax.axis_size(axis)
    pairs = [(i, i + by) for i in range(length) if 0 <= i + by < length]
    return lax.ppermute(value, axis, pairs)


def earlier_count(flags, axis):
    length = flags.shape[axis]
    at = jnp.arange(length)
    if axis == 0:
        before = (at[None, :] < at[:, None]).astype(jnp.float32)
        return jnp.dot(before, flags.astype(jnp.float32)).astype(jnp.int32)
    before = (at[:, None] < at[None, :]).astype(jnp.float32)
    return jnp.dot(flags.astype(jnp.float32), before).astype(jnp.int32)


def member_table(bucket_grid, owner, slot_count):
    matches = (bucket_grid == owner).astype(jnp.int32)
    ranking = earlier_count(matches, 1)
    slot_ids = jnp.arange(slot_count, dtype=jnp.int32)
    placed = matches[:, :, None] * (ranking[:, :, None] == slot_ids[None, None, :]).astype(
        jnp.int32
    )
    sources = bucket_grid.shape[0]
    stride = bucket_grid.shape[1]
    offsets = (
        jnp.arange(sources, dtype=jnp.int32)[:, None] * stride
        + jnp.arange(stride, dtype=jnp.int32)[None, :]
    )
    where_at = jnp.sum(placed * offsets[:, :, None], axis=1).reshape(-1)
    present = jnp.sum(placed, axis=1).reshape(-1)
    return (where_at, present)


def allowed_mask(where_here, alive_here, where_before, alive_before):
    amount = where_here.shape[0]
    asking = alive_here[:, None] > 0
    inside = (where_here[None, :] <= where_here[:, None]) & (alive_here[None, :] > 0) & asking
    inside = inside | (jnp.arange(amount)[:, None] == jnp.arange(amount)[None, :])
    earlier = (where_before[None, :] <= where_here[:, None]) & (alive_before[None, :] > 0) & asking
    return jnp.concatenate([inside, earlier], axis=1)


def softmax_rows(scores, allowed):
    masked = jnp.where(allowed[None], scores, -1e30)
    largest = jnp.max(masked, axis=2, keepdims=True)
    weights = jnp.where(allowed[None], jnp.exp(masked - largest), 0.0)
    return weights / jnp.sum(weights, axis=2, keepdims=True)


def local_slots(bucket_grid, device, sources, slot_total):
    my_buckets = lax.dynamic_index_in_dim(bucket_grid, device, 0, keepdims=False)
    owners = jnp.arange(sources, dtype=jnp.int32)
    onehot = (my_buckets[:, None] == owners[None, :]).astype(jnp.int32)
    ranking = jnp.sum(earlier_count(onehot, 0) * onehot, axis=1)
    back_index = my_buckets * slot_total + ranking
    slot_ids = jnp.arange(slot_total, dtype=jnp.int32)
    placed = onehot[:, :, None] * (ranking[:, None, None] == slot_ids[None, None, :]).astype(
        jnp.int32
    )
    token_ids = jnp.arange(my_buckets.shape[0], dtype=jnp.int32)
    send_index = jnp.sum(placed * token_ids[:, None, None], axis=0).reshape(-1)
    send_live = jnp.sum(placed, axis=0).reshape(-1)
    return (back_index, send_index, send_live)


def owner_probs(query_rows, key_all, allowed, scaling):
    scores = (
        jnp.einsum("qgd,kgd->gqk", query_rows, key_all, preferred_element_type=jnp.float32)
        * scaling
    )
    return softmax_rows(scores, allowed)


def owner_forward(probs, value_all):
    rounded = probs.astype(jnp.bfloat16)
    attended = jnp.einsum(
        "gqk,kgd->qgd", rounded, value_all, preferred_element_type=jnp.float32
    ).astype(jnp.bfloat16)
    return (rounded, attended)


def owner_backward(probs, rounded, attended, grad_rows, query_rows, key_all, value_all, scaling):
    centre = jnp.sum(attended.astype(jnp.float32) * grad_rows.astype(jnp.float32), axis=2)
    dprobs = jnp.einsum("qgd,kgd->gqk", grad_rows, value_all, preferred_element_type=jnp.float32)
    dscores = probs * (dprobs - jnp.transpose(centre)[:, :, None])
    dround = dscores.astype(jnp.bfloat16)
    grad_query = (
        jnp.einsum("gqk,kgd->qgd", dround, key_all, preferred_element_type=jnp.float32) * scaling
    ).astype(jnp.bfloat16)
    grad_key = (
        jnp.einsum("gqk,qgd->kgd", dround, query_rows, preferred_element_type=jnp.float32) * scaling
    )
    grad_value = jnp.einsum("gqk,qgd->kgd", rounded, grad_rows, preferred_element_type=jnp.float32)
    return (grad_query, grad_key, grad_value)


def with_previous(key_rows, value_rows):
    key_before, value_before = passed_along((key_rows, value_rows), "seq", 1)
    return (
        jnp.concatenate([key_rows, key_before], axis=0),
        jnp.concatenate([value_rows, value_before], axis=0),
    )


def settle_keys(grad_key, grad_value, slot_rows):
    key_next, value_next = passed_along(
        (grad_key[slot_rows:].astype(jnp.bfloat16), grad_value[slot_rows:].astype(jnp.bfloat16)),
        "seq",
        -1,
    )
    key_total = (grad_key[:slot_rows] + key_next.astype(jnp.float32)).astype(jnp.bfloat16)
    value_total = (grad_value[:slot_rows] + value_next.astype(jnp.float32)).astype(jnp.bfloat16)
    return (key_total, value_total)


def per_device(queries, keys, values, bucket, w_out, grad_out):
    sources = lax.axis_size("seq")
    device = lax.axis_index("seq")
    token_rows = queries.shape[0]
    features = queries.shape[1]
    groups = features // HSZ
    slot_total = max(2, 3 * token_rows // (2 * sources))
    slot_rows = sources * slot_total
    scaling = 1.0 / math.sqrt(HSZ)
    bucket_grid = bucket[:, 0].reshape(sources, token_rows)
    back_index, send_index, send_live = local_slots(bucket_grid, device, sources, slot_total)
    where_here, alive_here = member_table(bucket_grid, device, slot_total)
    where_before, alive_before = member_table(bucket_grid, device - 1, slot_total)
    allowed = allowed_mask(where_here, alive_here, where_before, alive_before)
    grad_heads = lax.dot_general(
        grad_out, w_out, (((1,), (1,)), ((), ())), preferred_element_type=jnp.float32
    ).astype(jnp.bfloat16)

    def pack_rows(source):
        return jnp.take(source, send_index, axis=0) * send_live[:, None].astype(source.dtype)

    def split_heads(block):
        return block.reshape(block.shape[0], groups, HSZ)

    def flatten(block):
        return block.reshape(block.shape[0], features)

    query_rows, key_rows, value_rows = (
        lax.all_to_all(pack_rows(queries), "seq", split_axis=0, concat_axis=0, tiled=True),
        lax.all_to_all(pack_rows(keys), "seq", split_axis=0, concat_axis=0, tiled=True),
        lax.all_to_all(pack_rows(values), "seq", split_axis=0, concat_axis=0, tiled=True),
    )
    key_all, value_all = with_previous(key_rows, value_rows)
    probs = owner_probs(split_heads(query_rows), split_heads(key_all), allowed, scaling)
    rounded, attended = owner_forward(probs, split_heads(value_all))
    key_all, value_all, probs, rounded, attended = (key_all, value_all, probs, rounded, attended)
    returned = lax.all_to_all(flatten(attended), "seq", split_axis=0, concat_axis=0, tiled=True)
    grad_rows = lax.all_to_all(
        pack_rows(grad_heads), "seq", split_axis=0, concat_axis=0, tiled=True
    )
    grad_query, grad_key, grad_value = owner_backward(
        probs,
        rounded,
        attended,
        split_heads(grad_rows),
        split_heads(query_rows),
        split_heads(key_all),
        split_heads(value_all),
        scaling,
    )
    key_total, value_total = settle_keys(flatten(grad_key), flatten(grad_value), slot_rows)
    back_query, back_key, back_value = (
        lax.all_to_all(flatten(grad_query), "seq", split_axis=0, concat_axis=0, tiled=True),
        lax.all_to_all(key_total, "seq", split_axis=0, concat_axis=0, tiled=True),
        lax.all_to_all(value_total, "seq", split_axis=0, concat_axis=0, tiled=True),
    )
    attended_home = jnp.take(returned, back_index, axis=0)
    partial_value = jnp.dot(attended_home, w_out, preferred_element_type=jnp.float32)
    layer_out = lax.psum_scatter(
        partial_value.astype(jnp.bfloat16), "head", scatter_dimension=1, tiled=True
    )
    weight_terms = lax.dot_general(
        attended_home, grad_out, (((0,), (0,)), ((), ())), preferred_element_type=jnp.float32
    )
    grad_weight = lax.psum_scatter(weight_terms, "seq", scatter_dimension=1, tiled=True)
    grad_queries = jnp.take(back_query, back_index, axis=0)
    grad_keys = jnp.take(back_key, back_index, axis=0)
    grad_values = jnp.take(back_value, back_index, axis=0)
    return (layer_out, grad_queries, grad_keys, grad_values, grad_weight)


MESH = pl.DeviceIdType.MESH
NT = (((1,), (1,)), ((), ()))
TN = (((0,), (0,)), ((), ()))


def times(a, b, dims):
    return lax.dot_general(a, b, dims, preferred_element_type=jnp.float32)


def dense_kernel(
    seqs,
    heads,
    q_hbm,
    k_hbm,
    v_hbm,
    brow,
    w_hbm,
    go_hbm,
    lo_out,
    gq_out,
    gk_out,
    gv_out,
    gw_out,
    w_buf,
    go_buf,
    gh_buf,
    q_buf,
    g_buf,
    k_buf,
    v_buf,
    go_all,
    att_all,
    dq_send,
    dk_acc,
    dv_acc,
    dk_send,
    dv_send,
    dq_in,
    dk_in,
    dv_in,
    dk_far,
    dv_far,
    lo_send,
    lo_in,
    local_sem,
    in_send,
    in_recv,
    far_send,
    far_recv,
    go_send,
    go_recv,
    gx_send,
    gx_recv,
    att_send,
    att_recv,
    attx_send,
    attx_recv,
    fwd_send,
    fwd_recv,
    dq_ssem,
    dq_rsem,
    dk_ssem,
    dk_rsem,
    dkf_ssem,
    dkf_rsem,
    lo_ssem,
    lo_rsem,
):
    s = lax.axis_index("seq")
    h = lax.axis_index("head")
    rows = q_hbm.shape[0]
    width = HSZ
    groups = q_hbm.shape[1] // width
    half = lax.div(s, groups)
    mine = lax.rem(s, groups)
    part = groups * rows
    scaling = 1.0 / math.sqrt(HSZ)
    gcols = w_hbm.shape[1] // seqs
    lcols = w_hbm.shape[1] // heads
    quarter = rows // heads
    low = half == 0
    high = half == 1

    def near(r):
        return lax.rem(mine + r, groups)

    def rows_of(block):
        return pl.ds(pl.multiple_of(block * rows, rows), rows)

    def cols_of(block, size=width):
        return pl.ds(pl.multiple_of(block * size, size), size)

    def remote(src, dst, ssem, rsem, where):
        return pltpu.make_async_remote_copy(
            src_ref=src, dst_ref=dst, send_sem=ssem, recv_sem=rsem, device_id=where,
            device_id_type=MESH,
        )

    w_copy = pltpu.make_async_copy(w_hbm, w_buf, local_sem.at[0])
    go_copy = pltpu.make_async_copy(go_hbm, go_buf, local_sem.at[1])
    go_copy.start()
    w_copy.start()
    own = [
        pltpu.make_async_copy(k_hbm.at[:, cols_of(mine)], k_buf.at[rows_of(s), :], local_sem.at[2]),
        pltpu.make_async_copy(v_hbm.at[:, cols_of(mine)], v_buf.at[rows_of(s), :], local_sem.at[3]),
        pltpu.make_async_copy(q_hbm.at[:, cols_of(mine)], q_buf.at[rows_of(mine), :], local_sem.at[4]),
    ]
    for copy in own:
        copy.start()
    quarter_rows = pl.ds(pl.multiple_of(h * quarter, quarter), quarter)
    go_own = pltpu.make_async_copy(
        go_hbm.at[quarter_rows, cols_of(s, gcols)], go_all.at[s, quarter_rows, :], local_sem.at[5]
    )
    go_own.start()

    barrier = pltpu.get_barrier_semaphore()
    for r in range(1, seqs):
        pl.semaphore_signal(
            barrier, inc=1, device_id=(lax.rem(s + r, seqs), h), device_id_type=MESH
        )
    for r in range(1, heads):
        pl.semaphore_signal(
            barrier, inc=1, device_id=(s, lax.rem(h + r, heads)), device_id_type=MESH
        )
    pl.semaphore_wait(barrier, seqs + heads - 2)

    far = []
    for r in range(groups):
        to = near(r)
        there = ((1 - half) * groups + to, h)
        for n, (src, dst) in enumerate(((k_hbm, k_buf), (v_hbm, v_buf))):
            far.append(
                remote(
                    src.at[:, cols_of(to)], dst.at[rows_of(s), :], far_send.at[r, n],
                    far_recv.at[r, n], there,
                )
            )

    inside = []
    for r in range(1, groups):
        to = near(r)
        there = (half * groups + to, h)
        for n, (src, dst, at) in enumerate(
            ((k_hbm, k_buf, s), (v_hbm, v_buf, s), (q_hbm, q_buf, mine))
        ):
            copy = remote(
                src.at[:, cols_of(to)], dst.at[rows_of(at), :], in_send.at[r, n],
                in_recv.at[r, n], there,
            )
            copy.start()
            inside.append(copy)

    @pl.when(low)
    def _():
        for copy in far:
            copy.start()
        k_buf[pl.ds(part, part), :] = jnp.zeros((part, width), k_buf.dtype)
        v_buf[pl.ds(part, part), :] = jnp.zeros((part, width), v_buf.dtype)

    @pl.when(high)
    def _():
        dk_far[...] = jnp.zeros_like(dk_far)
        dv_far[...] = jnp.zeros_like(dv_far)

    go_copy.wait()
    w_copy.wait()
    depth = w_buf.shape[1] // seqs

    def heads_step(c, total):
        at = pl.ds(pl.multiple_of(c * depth, depth), depth)
        return total + times(go_buf[:, at], w_buf[:, at], NT)

    gh = lax.fori_loop(
        0, seqs, heads_step, jnp.zeros((rows, groups * width), jnp.float32)
    )
    gh_buf[...] = gh.astype(jnp.bfloat16)
    for r in range(1, groups):
        to = near(r)
        copy = remote(
            gh_buf.at[:, cols_of(to)], g_buf.at[rows_of(mine), :], in_send.at[r, 3],
            in_recv.at[r, 3], (half * groups + to, h),
        )
        copy.start()
        inside.append(copy)
    g_buf[rows_of(mine), :] = gh_buf[:, cols_of(mine)]

    spread = []
    for r in range(1, seqs):
        to = lax.rem(s + r, seqs)
        copy = remote(
            go_hbm.at[quarter_rows, cols_of(to, gcols)], go_all.at[s, quarter_rows, :],
            go_send.at[r], go_recv.at[r], (to, h),
        )
        copy.start()
        spread.append(copy)

    for copy in own:
        copy.wait()
    for copy in inside:
        copy.wait_recv()

    @pl.when(high)
    def _():
        for copy in far:
            copy.wait_recv()

    keys_bucket = brow[...].astype(jnp.float32)
    diagonal = lax.broadcasted_iota(jnp.int32, (rows, rows), 0) == lax.broadcasted_iota(
        jnp.int32, (rows, rows), 1
    )
    keys_at = lax.broadcasted_iota(jnp.int32, (rows, seqs * rows), 1)
    exchange = []
    sent = []
    att_near = []
    att_cross = []
    dq_near = []
    order = list(range(1, groups)) + [0]
    for step, r in enumerate(order):
        block = near(r)
        token = half * groups + block
        qc = q_buf[rows_of(block), :]
        gc = g_buf[rows_of(block), :]
        k_all = k_buf[...]
        v_all = v_buf[...]
        along = brow[:, cols_of(token, rows)].astype(jnp.float32)
        gap = jnp.sum(jnp.where(diagonal, along, 0.0), axis=1, keepdims=True) - keys_bucket
        query_at = token * rows + lax.broadcasted_iota(jnp.int32, (rows, seqs * rows), 0)
        allowed = ((gap == 0.0) | (gap == 1.0)) & (keys_at <= query_at)
        scores = jnp.where(allowed, times(qc, k_all, NT) * scaling, -1e30)
        largest = jnp.max(scores, axis=1, keepdims=True)
        weights = jnp.where(allowed, jnp.exp(scores - largest), 0.0)
        probs = weights * (1.0 / jnp.sum(weights, axis=1, keepdims=True))
        rounded = probs.astype(jnp.bfloat16)
        attended = jnp.dot(rounded, v_all, preferred_element_type=jnp.float32).astype(jnp.bfloat16)
        att_all[rows_of(token), cols_of(mine)] = attended
        for n in range(1, groups):
            copy = remote(
                att_all.at[rows_of(token), cols_of(mine)],
                att_all.at[rows_of(token), cols_of(mine)],
                att_send.at[step, n], att_recv.at[step, n],
                (half * groups + near(n), h),
            )
            copy.start()
            att_near.append(copy)
        copy = remote(
            att_all.at[rows_of(token), cols_of(mine)],
            att_all.at[rows_of(token), cols_of(mine)],
            attx_send.at[step], attx_recv.at[step], ((1 - half) * groups + mine, h),
        )
        copy.start()
        att_cross.append(copy)
        centre = jnp.sum(
            attended.astype(jnp.float32) * gc.astype(jnp.float32), axis=1, keepdims=True
        )
        dscores = (probs * (times(gc, v_all, NT) - centre)).astype(jnp.bfloat16)
        dq = (jnp.dot(dscores, k_all, preferred_element_type=jnp.float32) * scaling).astype(
            jnp.bfloat16
        )
        if r == 0:
            dq_in[:, cols_of(mine)] = dq
        else:
            dq_send[r] = dq
            copy = remote(
                dq_send.at[r], dq_in.at[:, cols_of(mine)], dq_ssem.at[r], dq_rsem.at[r],
                (token, h),
            )
            copy.start()
            dq_near.append(copy)
        dk = times(dscores, qc, TN)
        dv = times(rounded, gc, TN)
        if step == 0:
            dk_acc[...] = dk
            dv_acc[...] = dv
        else:
            dk_acc[...] += dk
            dv_acc[...] += dv
        if step == 1:
            go_own.wait()
            for copy in spread:
                copy.wait_recv()
            for n in range(1, heads):
                copy = remote(
                    go_all.at[:, quarter_rows, :], go_all.at[:, quarter_rows, :],
                    gx_send.at[n], gx_recv.at[n], (s, lax.rem(h + n, heads)),
                )
                copy.start()
                exchange.append(copy)

    dk_send[...] = (dk_acc[...] * scaling).astype(jnp.bfloat16)
    dv_send[...] = dv_acc[...].astype(jnp.bfloat16)
    dk_cross = []
    for r in range(groups):
        to = near(r)
        for n, (src, dst) in enumerate(((dk_send, dk_far), (dv_send, dv_far))):
            dk_cross.append(
                remote(
                    src.at[rows_of(to), :], dst.at[:, cols_of(mine)], dkf_ssem.at[r, n],
                    dkf_rsem.at[r, n], ((1 - half) * groups + to, h),
                )
            )

    @pl.when(high)
    def _():
        for copy in dk_cross:
            copy.start()

    dk_near = []
    for r in range(1, groups):
        to = near(r)
        for n, (src, dst) in enumerate(((dk_send, dk_in), (dv_send, dv_in))):
            copy = remote(
                src.at[rows_of(half * groups + to), :], dst.at[:, cols_of(mine)],
                dk_ssem.at[r, n], dk_rsem.at[r, n], (half * groups + to, h),
            )
            copy.start()
            dk_near.append(copy)
    dk_in[:, cols_of(mine)] = dk_send[rows_of(s), :]
    dv_in[:, cols_of(mine)] = dv_send[rows_of(s), :]

    for copy in att_cross:
        copy.wait_recv()
    forward = []
    theirs = pl.ds(pl.multiple_of((1 - half) * part, part), part)
    for n in range(1, groups):
        copy = remote(
            att_all.at[theirs, cols_of(mine)], att_all.at[theirs, cols_of(mine)],
            fwd_send.at[n], fwd_recv.at[n], (half * groups + near(n), h),
        )
        copy.start()
        forward.append(copy)

    for copy in att_near:
        copy.wait_recv()
    home = att_all[rows_of(s), :]
    lo_near = []
    for n in range(1, heads):
        to = lax.rem(h + n, heads)
        lo_send[n] = jnp.dot(
            home, w_buf[:, cols_of(to, lcols)], preferred_element_type=jnp.float32
        ).astype(jnp.bfloat16)
        copy = remote(lo_send.at[n], lo_in.at[n], lo_ssem.at[n], lo_rsem.at[n], (s, to))
        copy.start()
        lo_near.append(copy)
    layer = jnp.dot(home, w_buf[:, cols_of(h, lcols)], preferred_element_type=jnp.float32)

    for copy in exchange:
        copy.wait_recv()
    for copy in dq_near:
        copy.wait_recv()
    gq_out[...] = dq_in[...]
    for n, copy in enumerate(lo_near):
        copy.wait_recv()
        layer = layer + lo_in[n + 1].astype(jnp.float32)
    lo_out[...] = layer.astype(jnp.bfloat16)
    for copy in forward:
        copy.wait_recv()
    gw = jnp.zeros(gw_out.shape, jnp.float32)
    for c in range(seqs):
        gw = gw + times(att_all[c * rows : (c + 1) * rows, :], go_all[c], TN)
    gw_out[...] = gw
    for copy in dk_near:
        copy.wait_recv()

    @pl.when(low)
    def _():
        for copy in dk_cross:
            copy.wait_recv()

    gk_out[...] = (dk_in[...].astype(jnp.float32) + dk_far[...].astype(jnp.float32)).astype(
        jnp.bfloat16
    )
    gv_out[...] = (dv_in[...].astype(jnp.float32) + dv_far[...].astype(jnp.float32)).astype(
        jnp.bfloat16
    )

    for copy in (
        inside + spread + exchange + att_near + att_cross + dq_near + dk_near + forward + lo_near
    ):
        copy.wait_send()

    @pl.when(low)
    def _():
        for copy in far:
            copy.wait_send()

    @pl.when(high)
    def _():
        for copy in dk_cross:
            copy.wait_send()


def place_kernel(*refs):
    sem = refs[-1]
    half = len(refs) // 2
    copies = [
        pltpu.make_async_copy(refs[n], refs[half + n], sem.at[n]) for n in range(half)
    ]
    for copy in copies:
        copy.start()
    for copy in copies:
        copy.wait()


def dense_device(queries, keys, values, bucket, w_out, grad_out):
    seqs = lax.axis_size("seq")
    heads = lax.axis_size("head")
    rows, features = queries.shape
    model = w_out.shape[1]
    groups = features // HSZ
    part = groups * rows
    tokens = seqs * rows
    bf, f32 = jnp.bfloat16, jnp.float32
    vmem = pl.BlockSpec(memory_space=pltpu.VMEM)
    hbm = pl.BlockSpec(memory_space=pl.ANY)
    dma = pltpu.SemaphoreType.DMA
    wide = pltpu.VMEM((rows, features), bf)
    sems = []
    for shape in (
        (groups, 4), (groups, 2), (seqs,), (heads,), (groups, groups), (groups,), (groups,),
        (groups,), (groups, 2), (groups, 2), (heads,),
    ):
        sems += [dma(shape), dma(shape)]
    shapes = (
        ((rows, model // heads), bf),
        ((rows, features), bf),
        ((rows, features), bf),
        ((rows, features), bf),
        ((features, model // seqs), f32),
    )
    made = pl.pallas_call(
        functools.partial(dense_kernel, seqs, heads),
        out_shape=tuple(pltpu.VMEM(shape, dtype) for shape, dtype in shapes),
        in_specs=[hbm, hbm, hbm, vmem, hbm, hbm],
        out_specs=(vmem,) * 5,
        scratch_shapes=[
            pltpu.VMEM(w_out.shape, bf),
            pltpu.VMEM(grad_out.shape, bf),
            wide,
            pltpu.VMEM((part, HSZ), bf),
            pltpu.VMEM((part, HSZ), bf),
            pltpu.VMEM((tokens, HSZ), bf),
            pltpu.VMEM((tokens, HSZ), bf),
            pltpu.VMEM((seqs, rows, model // seqs), bf),
            pltpu.VMEM((tokens, features), bf),
            pltpu.VMEM((groups, rows, HSZ), bf),
            pltpu.VMEM((tokens, HSZ), f32),
            pltpu.VMEM((tokens, HSZ), f32),
            pltpu.VMEM((tokens, HSZ), bf),
            pltpu.VMEM((tokens, HSZ), bf),
            wide,
            wide,
            wide,
            wide,
            wide,
            pltpu.VMEM((heads, rows, model // heads), bf),
            pltpu.VMEM((heads, rows, model // heads), bf),
            dma((6,)),
        ]
        + sems,
        compiler_params=pltpu.CompilerParams(
            collective_id=0, has_side_effects=True, vmem_limit_bytes=48 * 2**20
        ),
    )(queries, keys, values, bucket.reshape(1, -1), w_out, grad_out)
    return pl.pallas_call(
        place_kernel,
        out_shape=tuple(jax.ShapeDtypeStruct(shape, dtype) for shape, dtype in shapes),
        in_specs=[vmem] * 5,
        out_specs=(hbm,) * 5,
        scratch_shapes=[dma((5,))],
    )(*[pltpu.with_memory_space_constraint(one, pltpu.VMEM) for one in made])


def choose(queries, keys, values, bucket, w_out, grad_out):
    groups = queries.shape[1] // HSZ
    dense = lax.axis_size("seq") == 2 * groups
    plan = dense_device if dense else per_device
    return plan(queries, keys, values, bucket, w_out, grad_out)


def solution(mesh):
    return jax.shard_map(
        choose,
        mesh=mesh,
        in_specs=(
            P("seq", "head"),
            P("seq", "head"),
            P("seq", "head"),
            P(),
            P("head", None),
            P("seq", None),
        ),
        out_specs=(
            P("seq", "head"),
            P("seq", "head"),
            P("seq", "head"),
            P("seq", "head"),
            P("head", "seq"),
        ),
        check_vma=False,
    )
```

```python
import functools
import math

import jax
import jax.numpy as jnp
from jax import lax
from jax.experimental import pallas as pl
from jax.experimental.pallas import tpu as pltpu
from jax.sharding import PartitionSpec as P

HSZ = 128


def passed_along(value, axis, by):
    length = lax.axis_size(axis)
    pairs = [(i, i + by) for i in range(length) if 0 <= i + by < length]
    return lax.ppermute(value, axis, pairs)


def earlier_count(flags, axis):
    length = flags.shape[axis]
    at = jnp.arange(length)
    if axis == 0:
        before = (at[None, :] < at[:, None]).astype(jnp.float32)
        return jnp.dot(before, flags.astype(jnp.float32)).astype(jnp.int32)
    before = (at[:, None] < at[None, :]).astype(jnp.float32)
    return jnp.dot(flags.astype(jnp.float32), before).astype(jnp.int32)


def member_table(bucket_grid, owner, slot_count):
    matches = (bucket_grid == owner).astype(jnp.int32)
    ranking = earlier_count(matches, 1)
    slot_ids = jnp.arange(slot_count, dtype=jnp.int32)
    placed = matches[:, :, None] * (ranking[:, :, None] == slot_ids[None, None, :]).astype(
        jnp.int32
    )
    sources = bucket_grid.shape[0]
    stride = bucket_grid.shape[1]
    offsets = (
        jnp.arange(sources, dtype=jnp.int32)[:, None] * stride
        + jnp.arange(stride, dtype=jnp.int32)[None, :]
    )
    where_at = jnp.sum(placed * offsets[:, :, None], axis=1).reshape(-1)
    present = jnp.sum(placed, axis=1).reshape(-1)
    return (where_at, present)


def allowed_mask(where_here, alive_here, where_before, alive_before):
    amount = where_here.shape[0]
    asking = alive_here[:, None] > 0
    inside = (where_here[None, :] <= where_here[:, None]) & (alive_here[None, :] > 0) & asking
    inside = inside | (jnp.arange(amount)[:, None] == jnp.arange(amount)[None, :])
    earlier = (where_before[None, :] <= where_here[:, None]) & (alive_before[None, :] > 0) & asking
    return jnp.concatenate([inside, earlier], axis=1)


def softmax_rows(scores, allowed):
    masked = jnp.where(allowed[None], scores, -1e30)
    largest = jnp.max(masked, axis=2, keepdims=True)
    weights = jnp.where(allowed[None], jnp.exp(masked - largest), 0.0)
    return weights / jnp.sum(weights, axis=2, keepdims=True)


def local_slots(bucket_grid, device, sources, slot_total):
    my_buckets = lax.dynamic_index_in_dim(bucket_grid, device, 0, keepdims=False)
    owners = jnp.arange(sources, dtype=jnp.int32)
    onehot = (my_buckets[:, None] == owners[None, :]).astype(jnp.int32)
    ranking = jnp.sum(earlier_count(onehot, 0) * onehot, axis=1)
    back_index = my_buckets * slot_total + ranking
    slot_ids = jnp.arange(slot_total, dtype=jnp.int32)
    placed = onehot[:, :, None] * (ranking[:, None, None] == slot_ids[None, None, :]).astype(
        jnp.int32
    )
    token_ids = jnp.arange(my_buckets.shape[0], dtype=jnp.int32)
    send_index = jnp.sum(placed * token_ids[:, None, None], axis=0).reshape(-1)
    send_live = jnp.sum(placed, axis=0).reshape(-1)
    return (back_index, send_index, send_live)


def owner_probs(query_rows, key_all, allowed, scaling):
    scores = (
        jnp.einsum("qgd,kgd->gqk", query_rows, key_all, preferred_element_type=jnp.float32)
        * scaling
    )
    return softmax_rows(scores, allowed)


def owner_forward(probs, value_all):
    rounded = probs.astype(jnp.bfloat16)
    attended = jnp.einsum(
        "gqk,kgd->qgd", rounded, value_all, preferred_element_type=jnp.float32
    ).astype(jnp.bfloat16)
    return (rounded, attended)


def owner_backward(probs, rounded, attended, grad_rows, query_rows, key_all, value_all, scaling):
    centre = jnp.sum(attended.astype(jnp.float32) * grad_rows.astype(jnp.float32), axis=2)
    dprobs = jnp.einsum("qgd,kgd->gqk", grad_rows, value_all, preferred_element_type=jnp.float32)
    dscores = probs * (dprobs - jnp.transpose(centre)[:, :, None])
    dround = dscores.astype(jnp.bfloat16)
    grad_query = (
        jnp.einsum("gqk,kgd->qgd", dround, key_all, preferred_element_type=jnp.float32) * scaling
    ).astype(jnp.bfloat16)
    grad_key = (
        jnp.einsum("gqk,qgd->kgd", dround, query_rows, preferred_element_type=jnp.float32) * scaling
    )
    grad_value = jnp.einsum("gqk,qgd->kgd", rounded, grad_rows, preferred_element_type=jnp.float32)
    return (grad_query, grad_key, grad_value)


def with_previous(key_rows, value_rows):
    key_before, value_before = passed_along((key_rows, value_rows), "seq", 1)
    return (
        jnp.concatenate([key_rows, key_before], axis=0),
        jnp.concatenate([value_rows, value_before], axis=0),
    )


def settle_keys(grad_key, grad_value, slot_rows):
    key_next, value_next = passed_along(
        (grad_key[slot_rows:].astype(jnp.bfloat16), grad_value[slot_rows:].astype(jnp.bfloat16)),
        "seq",
        -1,
    )
    key_total = (grad_key[:slot_rows] + key_next.astype(jnp.float32)).astype(jnp.bfloat16)
    value_total = (grad_value[:slot_rows] + value_next.astype(jnp.float32)).astype(jnp.bfloat16)
    return (key_total, value_total)


def per_device(queries, keys, values, bucket, w_out, grad_out):
    sources = lax.axis_size("seq")
    device = lax.axis_index("seq")
    token_rows = queries.shape[0]
    features = queries.shape[1]
    groups = features // HSZ
    slot_total = max(2, 3 * token_rows // (2 * sources))
    slot_rows = sources * slot_total
    scaling = 1.0 / math.sqrt(HSZ)
    bucket_grid = bucket[:, 0].reshape(sources, token_rows)
    back_index, send_index, send_live = local_slots(bucket_grid, device, sources, slot_total)
    where_here, alive_here = member_table(bucket_grid, device, slot_total)
    where_before, alive_before = member_table(bucket_grid, device - 1, slot_total)
    allowed = allowed_mask(where_here, alive_here, where_before, alive_before)
    grad_heads = lax.dot_general(
        grad_out, w_out, (((1,), (1,)), ((), ())), preferred_element_type=jnp.float32
    ).astype(jnp.bfloat16)

    def pack_rows(source):
        return jnp.take(source, send_index, axis=0) * send_live[:, None].astype(source.dtype)

    def split_heads(block):
        return block.reshape(block.shape[0], groups, HSZ)

    def flatten(block):
        return block.reshape(block.shape[0], features)

    query_rows, key_rows, value_rows = (
        lax.all_to_all(pack_rows(queries), "seq", split_axis=0, concat_axis=0, tiled=True),
        lax.all_to_all(pack_rows(keys), "seq", split_axis=0, concat_axis=0, tiled=True),
        lax.all_to_all(pack_rows(values), "seq", split_axis=0, concat_axis=0, tiled=True),
    )
    key_all, value_all = with_previous(key_rows, value_rows)
    probs = owner_probs(split_heads(query_rows), split_heads(key_all), allowed, scaling)
    rounded, attended = owner_forward(probs, split_heads(value_all))
    key_all, value_all, probs, rounded, attended = (key_all, value_all, probs, rounded, attended)
    returned = lax.all_to_all(flatten(attended), "seq", split_axis=0, concat_axis=0, tiled=True)
    grad_rows = lax.all_to_all(
        pack_rows(grad_heads), "seq", split_axis=0, concat_axis=0, tiled=True
    )
    grad_query, grad_key, grad_value = owner_backward(
        probs,
        rounded,
        attended,
        split_heads(grad_rows),
        split_heads(query_rows),
        split_heads(key_all),
        split_heads(value_all),
        scaling,
    )
    key_total, value_total = settle_keys(flatten(grad_key), flatten(grad_value), slot_rows)
    back_query, back_key, back_value = (
        lax.all_to_all(flatten(grad_query), "seq", split_axis=0, concat_axis=0, tiled=True),
        lax.all_to_all(key_total, "seq", split_axis=0, concat_axis=0, tiled=True),
        lax.all_to_all(value_total, "seq", split_axis=0, concat_axis=0, tiled=True),
    )
    attended_home = jnp.take(returned, back_index, axis=0)
    partial_value = jnp.dot(attended_home, w_out, preferred_element_type=jnp.float32)
    layer_out = lax.psum_scatter(
        partial_value.astype(jnp.bfloat16), "head", scatter_dimension=1, tiled=True
    )
    weight_terms = lax.dot_general(
        attended_home, grad_out, (((0,), (0,)), ((), ())), preferred_element_type=jnp.float32
    )
    grad_weight = lax.psum_scatter(weight_terms, "seq", scatter_dimension=1, tiled=True)
    grad_queries = jnp.take(back_query, back_index, axis=0)
    grad_keys = jnp.take(back_key, back_index, axis=0)
    grad_values = jnp.take(back_value, back_index, axis=0)
    return (layer_out, grad_queries, grad_keys, grad_values, grad_weight)


MESH = pl.DeviceIdType.MESH
NT = (((1,), (1,)), ((), ()))
TN = (((0,), (0,)), ((), ()))


def times(a, b, dims):
    return lax.dot_general(a, b, dims, preferred_element_type=jnp.float32)


def dense_kernel(
    seqs,
    heads,
    q_hbm,
    k_hbm,
    v_hbm,
    brow,
    w_hbm,
    go_hbm,
    lo_out,
    gq_out,
    gk_out,
    gv_out,
    gw_out,
    w_buf,
    go_buf,
    gh_buf,
    q_buf,
    g_buf,
    k_buf,
    v_buf,
    go_all,
    att_all,
    dq_send,
    dk_acc,
    dv_acc,
    dk_send,
    dv_send,
    dq_in,
    dk_in,
    dv_in,
    dk_far,
    dv_far,
    lo_send,
    lo_in,
    p_buf,
    local_sem,
    in_send,
    in_recv,
    far_send,
    far_recv,
    go_send,
    go_recv,
    gx_send,
    gx_recv,
    att_send,
    att_recv,
    fwd_send,
    fwd_recv,
    dq_ssem,
    dq_rsem,
    dk_ssem,
    dk_rsem,
    dkf_ssem,
    dkf_rsem,
    lo_ssem,
    lo_rsem,
):
    s = lax.axis_index("seq")
    h = lax.axis_index("head")
    rows = q_hbm.shape[0]
    width = HSZ
    groups = q_hbm.shape[1] // width
    half = lax.div(s, groups)
    mine = lax.rem(s, groups)
    part = groups * rows
    scaling = 1.0 / math.sqrt(HSZ)
    gcols = w_hbm.shape[1] // seqs
    lcols = w_hbm.shape[1] // heads
    quarter = rows // heads
    low = half == 0
    high = half == 1
    deep = lax.div(mine, 2)

    def flip(index, bits):
        out = index
        for bit in (1, 2, 4):
            if bits & bit:
                out = out + bit * (1 - 2 * lax.rem(lax.div(index, bit), 2))
        return out

    def near(r):
        return flip(mine, r)

    def rows_of(block):
        return pl.ds(pl.multiple_of(block * rows, rows), rows)

    def cols_of(block, size=width):
        return pl.ds(pl.multiple_of(block * size, size), size)

    def quarter_of(head):
        return pl.ds(pl.multiple_of(head * quarter, quarter), quarter)

    def remote(src, dst, ssem, rsem, where):
        return pltpu.make_async_remote_copy(
            src_ref=src, dst_ref=dst, send_sem=ssem, recv_sem=rsem, device_id=where,
            device_id_type=MESH,
        )

    x_to, z_to, d_to = (flip(s, 1), h), (flip(s, 2), h), (flip(s, 3), h)
    c_to = (flip(s, 4), h)
    core_to, y_to = (s, flip(h, 1)), (s, flip(h, 2))

    w_copy = pltpu.make_async_copy(w_hbm, w_buf, local_sem.at[0])
    go_copy = pltpu.make_async_copy(go_hbm, go_buf, local_sem.at[1])
    go_copy.start()
    w_copy.start()
    own = [
        pltpu.make_async_copy(k_hbm.at[:, cols_of(mine)], k_buf.at[rows_of(s), :], local_sem.at[2]),
        pltpu.make_async_copy(v_hbm.at[:, cols_of(mine)], v_buf.at[rows_of(s), :], local_sem.at[3]),
        pltpu.make_async_copy(q_hbm.at[:, cols_of(mine)], q_buf.at[rows_of(mine), :], local_sem.at[4]),
    ]
    for copy in own:
        copy.start()
    go_own = pltpu.make_async_copy(
        go_hbm.at[quarter_of(h), cols_of(s, gcols)], go_all.at[s, quarter_of(h), :], local_sem.at[5]
    )
    go_own.start()

    barrier = pltpu.get_barrier_semaphore()
    for r in range(1, seqs):
        pl.semaphore_signal(
            barrier, inc=1, device_id=(lax.rem(s + r, seqs), h), device_id_type=MESH
        )
    for there in (core_to, y_to):
        pl.semaphore_signal(barrier, inc=1, device_id=there, device_id_type=MESH)
    pl.semaphore_wait(barrier, seqs + 1)

    def cross_copies(sources, there_in, ssem, rsem):
        out = []
        for block in range(2):
            for side in range(2):
                to = 2 * block + lax.rem(mine + side, 2)
                for n, (src, dst) in enumerate(sources):
                    out.append(
                        remote(
                            src(to), dst, ssem.at[2 * block + side, n],
                            rsem.at[2 * deep + side, n], ((1 - half) * groups + to, there_in),
                        )
                    )
        return out

    def cross_arrivals(sources, ssem, rsem):
        return [
            remote(src(mine), dst, ssem.at[r, n], rsem.at[r, n], c_to)
            for r in range(groups)
            for n, (src, dst) in enumerate(sources)
        ]

    far_sources = (
        (lambda to: k_hbm.at[:, cols_of(to)], k_buf.at[rows_of(s), :]),
        (lambda to: v_hbm.at[:, cols_of(to)], v_buf.at[rows_of(s), :]),
    )
    far = cross_copies(far_sources, h, far_send, far_recv)
    far_in = cross_arrivals(far_sources, far_send, far_recv)

    @pl.when(low)
    def _():
        for copy in far[:4]:
            copy.start()

    inside = []
    for n, (src, dst, at) in enumerate(
        ((k_hbm, k_buf, s), (q_hbm, q_buf, mine), (v_hbm, v_buf, s))
    ):
        for r in (3, 2, 1):
            to = near(r)
            copy = remote(
                src.at[:, cols_of(to)], dst.at[rows_of(at), :], in_send.at[r, n],
                in_recv.at[r, n], (half * groups + to, h),
            )
            copy.start()
            inside.append(copy)
    spread = []
    for r in range(1, seqs):
        to = lax.rem(s + r, seqs)
        spread.append(
            remote(
                go_hbm.at[quarter_of(h), cols_of(to, gcols)], go_all.at[s, quarter_of(h), :],
                go_send.at[r], go_recv.at[r], (to, h),
            )
        )

    @pl.when(low)
    def _():
        for copy in far[4:]:
            copy.start()

    @pl.when(high)
    def _():
        for copy in spread:
            copy.start()

    @pl.when(low)
    def _():
        k_buf[pl.ds(part, part), :] = jnp.zeros((part, width), k_buf.dtype)
        v_buf[pl.ds(part, part), :] = jnp.zeros((part, width), v_buf.dtype)

    @pl.when(high)
    def _():
        dk_far[...] = jnp.zeros_like(dk_far)
        dv_far[...] = jnp.zeros_like(dv_far)

    go_copy.wait()
    w_copy.wait()
    depth = w_buf.shape[1] // seqs

    def heads_step(c, total):
        at = pl.ds(pl.multiple_of(c * depth, depth), depth)
        return total + times(go_buf[:, at], w_buf[:, at], NT)

    gh = lax.fori_loop(
        0, seqs, heads_step, jnp.zeros((rows, groups * width), jnp.float32)
    )
    gh_buf[...] = gh.astype(jnp.bfloat16)
    gh_near = []
    for r in (3, 2, 1):
        to = near(r)
        copy = remote(
            gh_buf.at[:, cols_of(to)], g_buf.at[rows_of(mine), :], in_send.at[r, 3],
            in_recv.at[r, 3], (half * groups + to, h),
        )
        copy.start()
        gh_near.append(copy)
    g_buf[rows_of(mine), :] = gh_buf[:, cols_of(mine)]

    @pl.when(low)
    def _():
        for copy in spread:
            copy.start()

    for copy in own:
        copy.wait()
    for copy in inside:
        copy.wait_recv()

    @pl.when(high)
    def _():
        for copy in far_in:
            copy.wait_recv()

    def piece(token, head, kind, there):
        at = att_all.at[rows_of(token), cols_of(head)]
        lane, step = kind
        return remote(at, at, att_send.at[lane, step], att_recv.at[lane, step], there)

    def onward(token, head, kind, there):
        at = att_all.at[rows_of(token), cols_of(head)]
        lane, step = kind
        return remote(at, at, fwd_send.at[lane, step], fwd_recv.at[lane, step], there)

    keys_bucket = brow[...].astype(jnp.float32)
    diagonal = lax.broadcasted_iota(jnp.int32, (rows, rows), 0) == lax.broadcasted_iota(
        jnp.int32, (rows, rows), 1
    )
    keys_at = lax.broadcasted_iota(jnp.int32, (rows, seqs * rows), 1)
    order = (3, 1, 2, 0)
    go_moves = [
        remote(
            go_all.at[:, quarter_of(h), :], go_all.at[:, quarter_of(h), :],
            gx_send.at[0], gx_recv.at[0], y_to,
        ),
        remote(
            go_all.at[:, quarter_of(h), :], go_all.at[:, quarter_of(h), :],
            gx_send.at[1], gx_recv.at[1], core_to,
        ),
        remote(
            go_all.at[:, quarter_of(flip(h, 2)), :], go_all.at[:, quarter_of(flip(h, 2)), :],
            gx_send.at[2], gx_recv.at[2], core_to,
        ),
    ]
    att_x, att_z, att_c, att_d = {}, {}, {}, {}
    dq_near = []
    for step, r in enumerate(order):
        block = near(r)
        token = half * groups + block
        qc = q_buf[rows_of(block), :]
        k_all = k_buf[...]
        v_all = v_buf[...]
        along = brow[:, cols_of(token, rows)].astype(jnp.float32)
        gap = jnp.sum(jnp.where(diagonal, along, 0.0), axis=1, keepdims=True) - keys_bucket
        query_at = token * rows + lax.broadcasted_iota(jnp.int32, (rows, seqs * rows), 0)
        allowed = ((gap == 0.0) | (gap == 1.0)) & (keys_at <= query_at)
        scores = jnp.where(allowed, times(qc, k_all, NT) * scaling, -1e30)
        largest = jnp.max(scores, axis=1, keepdims=True)
        weights = jnp.where(allowed, jnp.exp(scores - largest), 0.0)
        probs = weights * (1.0 / jnp.sum(weights, axis=1, keepdims=True))
        p_buf[step] = probs
        attended = jnp.dot(
            probs.astype(jnp.bfloat16), v_all, preferred_element_type=jnp.float32
        ).astype(jnp.bfloat16)
        att_all[rows_of(token), cols_of(mine)] = attended
        if r == 3:
            att_d[r] = piece(token, mine, (3, step), d_to)
            att_d[r].start()
        att_c[r] = piece(token, mine, (2, step), c_to)
        att_z[r] = piece(token, mine, (1, step), z_to)
        att_x[r] = piece(token, mine, (0, step), x_to)
        for copy in (att_z[r], att_x[r], att_c[r]):
            copy.start()

    cross_z, cross_x = {}, {}
    for step, r in enumerate(order):
        token = (1 - half) * groups + near(r)
        cross_z[r] = onward(token, mine, (1, step), z_to)
        cross_x[r] = onward(token, mine, (2, step), x_to)

    def pass_cross():
        for r in order:
            att_c[r].wait_recv()
            cross_z[r].start()
            cross_x[r].start()

    @pl.when(half + deep == 2)
    def _():
        pass_cross()

    for copy in gh_near:
        copy.wait_recv()
    for step, r in enumerate(order):
        block = near(r)
        token = half * groups + block
        qc = q_buf[rows_of(block), :]
        gc = g_buf[rows_of(block), :]
        k_all = k_buf[...]
        v_all = v_buf[...]
        probs = p_buf[step]
        rounded = probs.astype(jnp.bfloat16)
        attended = att_all[rows_of(token), cols_of(mine)]
        centre = jnp.sum(
            attended.astype(jnp.float32) * gc.astype(jnp.float32), axis=1, keepdims=True
        )
        dscores = (probs * (times(gc, v_all, NT) - centre)).astype(jnp.bfloat16)
        dq = (jnp.dot(dscores, k_all, preferred_element_type=jnp.float32) * scaling).astype(
            jnp.bfloat16
        )
        if r == 0:
            dq_in[:, cols_of(mine)] = dq
        else:
            dq_send[r] = dq
            copy = remote(
                dq_send.at[r], dq_in.at[:, cols_of(mine)], dq_ssem.at[r], dq_rsem.at[r],
                (token, h),
            )
            copy.start()
            dq_near.append(copy)
        dk = times(dscores, qc, TN)
        dv = times(rounded, gc, TN)
        if step == 0:
            dk_acc[...] = dk
            dv_acc[...] = dv
        else:
            dk_acc[...] += dk
            dv_acc[...] += dv
        if step == 0:
            go_own.wait()
            for copy in spread:
                copy.wait_recv()
            go_moves[0].start()
            go_moves[1].start()

    dk_send[...] = (dk_acc[...] * scaling).astype(jnp.bfloat16)
    dv_send[...] = dv_acc[...].astype(jnp.bfloat16)
    dk_sources = (
        (lambda to: dk_send.at[rows_of(to), :], dk_far.at[:, cols_of(mine)]),
        (lambda to: dv_send.at[rows_of(to), :], dv_far.at[:, cols_of(mine)]),
    )
    dk_cross = cross_copies(dk_sources, h, dkf_ssem, dkf_rsem)
    dk_cross_in = cross_arrivals(dk_sources, dkf_ssem, dkf_rsem)

    @pl.when(high)
    def _():
        for copy in dk_cross:
            copy.start()

    dk_near = []
    for r in range(1, groups):
        to = near(r)
        for n, (src, dst) in enumerate(((dk_send, dk_in), (dv_send, dv_in))):
            copy = remote(
                src.at[rows_of(half * groups + to), :], dst.at[:, cols_of(mine)],
                dk_ssem.at[r, n], dk_rsem.at[r, n], (half * groups + to, h),
            )
            copy.start()
            dk_near.append(copy)
    dk_in[:, cols_of(mine)] = dk_send[rows_of(s), :]
    dv_in[:, cols_of(mine)] = dv_send[rows_of(s), :]

    def own_token(bits):
        return half * groups + near(bits)

    def other_token(bits):
        return (1 - half) * groups + near(bits)

    @pl.when((half == 1) & (deep == 0))
    def _():
        pass_cross()

    fwd_near = {}
    for step, r in enumerate(order):
        if r != 3:
            fwd_near[r] = onward(own_token(2 ^ r), near(2), (0, step), x_to)
            att_z[r].wait_recv()
            fwd_near[r].start()
    go_moves[0].wait_recv()
    go_moves[2].start()

    att_x[1].wait_recv()
    att_d[3].wait_recv()
    home = att_all[rows_of(s), :]

    def partial_for(head):
        return jnp.dot(home, w_buf[:, cols_of(head, lcols)], preferred_element_type=jnp.float32)

    lo_moves = [
        remote(lo_send.at[0], lo_in.at[0], lo_ssem.at[0], lo_rsem.at[0], core_to),
        remote(lo_send.at[1], lo_in.at[1], lo_ssem.at[1], lo_rsem.at[1], core_to),
        remote(lo_send.at[2], lo_in.at[2], lo_ssem.at[2], lo_rsem.at[2], y_to),
    ]
    lo_send[0] = partial_for(flip(h, 3)).astype(jnp.bfloat16)
    lo_moves[0].start()
    across = partial_for(flip(h, 2))
    lo_moves[0].wait_recv()
    lo_send[2] = (across + lo_in[0].astype(jnp.float32)).astype(jnp.bfloat16)
    lo_moves[2].start()
    lo_send[1] = partial_for(flip(h, 1)).astype(jnp.bfloat16)
    lo_moves[1].start()
    layer = partial_for(h)

    @pl.when(low)
    def _():
        pass_cross()

    cross_on = {}
    for step, r in enumerate(order):
        cross_on[r] = onward(other_token(2 ^ r), near(2), (3, step), x_to)
        cross_z[r].wait_recv()
        cross_on[r].start()

    def weight_rows(bits):
        head = near(bits)
        gw_out[rows_of(head), :] = times(
            att_all[:, cols_of(head)], go_all[...].reshape(seqs * rows, gcols), TN
        )

    go_moves[1].wait_recv()
    go_moves[2].wait_recv()
    weight_rows(0)
    att_z[3].wait_recv()
    weight_rows(2)
    for copy in dq_near:
        copy.wait_recv()
    gq_out[...] = dq_in[...]
    lo_moves[1].wait_recv()
    lo_moves[2].wait_recv()
    lo_out[...] = (layer + lo_in[1].astype(jnp.float32) + lo_in[2].astype(jnp.float32)).astype(
        jnp.bfloat16
    )
    for r in order:
        if r != 1:
            att_x[r].wait_recv()
        cross_x[r].wait_recv()
    weight_rows(1)
    for copy in dk_near:
        copy.wait_recv()

    @pl.when(low)
    def _():
        for copy in dk_cross_in:
            copy.wait_recv()

    gk_out[...] = (dk_in[...].astype(jnp.float32) + dk_far[...].astype(jnp.float32)).astype(
        jnp.bfloat16
    )
    gv_out[...] = (dv_in[...].astype(jnp.float32) + dv_far[...].astype(jnp.float32)).astype(
        jnp.bfloat16
    )
    for r in order:
        if r != 3:
            fwd_near[r].wait_recv()
        cross_on[r].wait_recv()
    weight_rows(3)

    moved = inside + gh_near + spread + go_moves + dq_near + dk_near + lo_moves
    for group in (att_x, att_z, att_c, att_d, fwd_near, cross_z, cross_x, cross_on):
        moved += list(group.values())
    for copy in moved:
        copy.wait_send()

    @pl.when(low)
    def _():
        for copy in far:
            copy.wait_send()

    @pl.when(high)
    def _():
        for copy in dk_cross:
            copy.wait_send()


def place_kernel(*refs):
    sem = refs[-1]
    half = len(refs) // 2
    copies = [
        pltpu.make_async_copy(refs[n], refs[half + n], sem.at[n]) for n in range(half)
    ]
    for copy in copies:
        copy.start()
    for copy in copies:
        copy.wait()


def dense_device(queries, keys, values, bucket, w_out, grad_out):
    seqs = lax.axis_size("seq")
    heads = lax.axis_size("head")
    rows, features = queries.shape
    model = w_out.shape[1]
    groups = features // HSZ
    part = groups * rows
    tokens = seqs * rows
    bf, f32 = jnp.bfloat16, jnp.float32
    vmem = pl.BlockSpec(memory_space=pltpu.VMEM)
    hbm = pl.BlockSpec(memory_space=pl.ANY)
    dma = pltpu.SemaphoreType.DMA
    wide = pltpu.VMEM((rows, features), bf)
    sems = []
    for shape in (
        (groups, 4), (groups, 2), (seqs,), (3,), (4, groups), (4, groups), (groups,), (groups, 2),
        (groups, 2), (3,),
    ):
        sems += [dma(shape), dma(shape)]
    shapes = (
        ((rows, model // heads), bf),
        ((rows, features), bf),
        ((rows, features), bf),
        ((rows, features), bf),
        ((features, model // seqs), f32),
    )
    made = pl.pallas_call(
        functools.partial(dense_kernel, seqs, heads),
        out_shape=tuple(pltpu.VMEM(shape, dtype) for shape, dtype in shapes),
        in_specs=[hbm, hbm, hbm, vmem, hbm, hbm],
        out_specs=(vmem,) * 5,
        scratch_shapes=[
            pltpu.VMEM(w_out.shape, bf),
            pltpu.VMEM(grad_out.shape, bf),
            wide,
            pltpu.VMEM((part, HSZ), bf),
            pltpu.VMEM((part, HSZ), bf),
            pltpu.VMEM((tokens, HSZ), bf),
            pltpu.VMEM((tokens, HSZ), bf),
            pltpu.VMEM((seqs, rows, model // seqs), bf),
            pltpu.VMEM((tokens, features), bf),
            pltpu.VMEM((groups, rows, HSZ), bf),
            pltpu.VMEM((tokens, HSZ), f32),
            pltpu.VMEM((tokens, HSZ), f32),
            pltpu.VMEM((tokens, HSZ), bf),
            pltpu.VMEM((tokens, HSZ), bf),
            wide,
            wide,
            wide,
            wide,
            wide,
            pltpu.VMEM((3, rows, model // heads), bf),
            pltpu.VMEM((3, rows, model // heads), bf),
            pltpu.VMEM((groups, rows, tokens), f32),
            dma((6,)),
        ]
        + sems,
        compiler_params=pltpu.CompilerParams(
            collective_id=0, has_side_effects=True, vmem_limit_bytes=58 * 2**20
        ),
    )(queries, keys, values, bucket.reshape(1, -1), w_out, grad_out)
    return pl.pallas_call(
        place_kernel,
        out_shape=tuple(jax.ShapeDtypeStruct(shape, dtype) for shape, dtype in shapes),
        in_specs=[vmem] * 5,
        out_specs=(hbm,) * 5,
        scratch_shapes=[dma((5,))],
    )(*[pltpu.with_memory_space_constraint(one, pltpu.VMEM) for one in made])


def choose(queries, keys, values, bucket, w_out, grad_out):
    groups = queries.shape[1] // HSZ
    dense = groups == 4 and lax.axis_size("seq") == 8 and lax.axis_size("head") == 4
    plan = dense_device if dense else per_device
    return plan(queries, keys, values, bucket, w_out, grad_out)


def solution(mesh):
    return jax.shard_map(
        choose,
        mesh=mesh,
        in_specs=(
            P("seq", "head"),
            P("seq", "head"),
            P("seq", "head"),
            P(),
            P("head", None),
            P("seq", None),
        ),
        out_specs=(
            P("seq", "head"),
            P("seq", "head"),
            P("seq", "head"),
            P("seq", "head"),
            P("head", "seq"),
        ),
        check_vma=False,
    )
```

```python
import functools
import math

import jax
import jax.numpy as jnp
from jax import lax
from jax.experimental import pallas as pl
from jax.experimental.pallas import tpu as pltpu
from jax.sharding import PartitionSpec as P

HSZ = 128


def passed_along(value, axis, by):
    length = lax.axis_size(axis)
    pairs = [(i, i + by) for i in range(length) if 0 <= i + by < length]
    return lax.ppermute(value, axis, pairs)


def earlier_count(flags, axis):
    length = flags.shape[axis]
    at = jnp.arange(length)
    if axis == 0:
        before = (at[None, :] < at[:, None]).astype(jnp.float32)
        return jnp.dot(before, flags.astype(jnp.float32)).astype(jnp.int32)
    before = (at[:, None] < at[None, :]).astype(jnp.float32)
    return jnp.dot(flags.astype(jnp.float32), before).astype(jnp.int32)


def member_table(bucket_grid, owner, slot_count):
    matches = (bucket_grid == owner).astype(jnp.int32)
    ranking = earlier_count(matches, 1)
    slot_ids = jnp.arange(slot_count, dtype=jnp.int32)
    placed = matches[:, :, None] * (ranking[:, :, None] == slot_ids[None, None, :]).astype(
        jnp.int32
    )
    sources = bucket_grid.shape[0]
    stride = bucket_grid.shape[1]
    offsets = (
        jnp.arange(sources, dtype=jnp.int32)[:, None] * stride
        + jnp.arange(stride, dtype=jnp.int32)[None, :]
    )
    where_at = jnp.sum(placed * offsets[:, :, None], axis=1).reshape(-1)
    present = jnp.sum(placed, axis=1).reshape(-1)
    return (where_at, present)


def allowed_mask(where_here, alive_here, where_before, alive_before):
    amount = where_here.shape[0]
    asking = alive_here[:, None] > 0
    inside = (where_here[None, :] <= where_here[:, None]) & (alive_here[None, :] > 0) & asking
    inside = inside | (jnp.arange(amount)[:, None] == jnp.arange(amount)[None, :])
    earlier = (where_before[None, :] <= where_here[:, None]) & (alive_before[None, :] > 0) & asking
    return jnp.concatenate([inside, earlier], axis=1)


def softmax_rows(scores, allowed):
    masked = jnp.where(allowed[None], scores, -1e30)
    largest = jnp.max(masked, axis=2, keepdims=True)
    weights = jnp.where(allowed[None], jnp.exp(masked - largest), 0.0)
    return weights / jnp.sum(weights, axis=2, keepdims=True)


def local_slots(bucket_grid, device, sources, slot_total):
    my_buckets = lax.dynamic_index_in_dim(bucket_grid, device, 0, keepdims=False)
    owners = jnp.arange(sources, dtype=jnp.int32)
    onehot = (my_buckets[:, None] == owners[None, :]).astype(jnp.int32)
    ranking = jnp.sum(earlier_count(onehot, 0) * onehot, axis=1)
    back_index = my_buckets * slot_total + ranking
    slot_ids = jnp.arange(slot_total, dtype=jnp.int32)
    placed = onehot[:, :, None] * (ranking[:, None, None] == slot_ids[None, None, :]).astype(
        jnp.int32
    )
    token_ids = jnp.arange(my_buckets.shape[0], dtype=jnp.int32)
    send_index = jnp.sum(placed * token_ids[:, None, None], axis=0).reshape(-1)
    send_live = jnp.sum(placed, axis=0).reshape(-1)
    return (back_index, send_index, send_live)


def owner_probs(query_rows, key_all, allowed, scaling):
    scores = (
        jnp.einsum("qgd,kgd->gqk", query_rows, key_all, preferred_element_type=jnp.float32)
        * scaling
    )
    return softmax_rows(scores, allowed)


def owner_forward(probs, value_all):
    rounded = probs.astype(jnp.bfloat16)
    attended = jnp.einsum(
        "gqk,kgd->qgd", rounded, value_all, preferred_element_type=jnp.float32
    ).astype(jnp.bfloat16)
    return (rounded, attended)


def owner_backward(probs, rounded, attended, grad_rows, query_rows, key_all, value_all, scaling):
    centre = jnp.sum(attended.astype(jnp.float32) * grad_rows.astype(jnp.float32), axis=2)
    dprobs = jnp.einsum("qgd,kgd->gqk", grad_rows, value_all, preferred_element_type=jnp.float32)
    dscores = probs * (dprobs - jnp.transpose(centre)[:, :, None])
    dround = dscores.astype(jnp.bfloat16)
    grad_query = (
        jnp.einsum("gqk,kgd->qgd", dround, key_all, preferred_element_type=jnp.float32) * scaling
    ).astype(jnp.bfloat16)
    grad_key = (
        jnp.einsum("gqk,qgd->kgd", dround, query_rows, preferred_element_type=jnp.float32) * scaling
    )
    grad_value = jnp.einsum("gqk,qgd->kgd", rounded, grad_rows, preferred_element_type=jnp.float32)
    return (grad_query, grad_key, grad_value)


def with_previous(key_rows, value_rows):
    key_before, value_before = passed_along((key_rows, value_rows), "seq", 1)
    return (
        jnp.concatenate([key_rows, key_before], axis=0),
        jnp.concatenate([value_rows, value_before], axis=0),
    )


def settle_keys(grad_key, grad_value, slot_rows):
    key_next, value_next = passed_along(
        (grad_key[slot_rows:].astype(jnp.bfloat16), grad_value[slot_rows:].astype(jnp.bfloat16)),
        "seq",
        -1,
    )
    key_total = (grad_key[:slot_rows] + key_next.astype(jnp.float32)).astype(jnp.bfloat16)
    value_total = (grad_value[:slot_rows] + value_next.astype(jnp.float32)).astype(jnp.bfloat16)
    return (key_total, value_total)


def per_device(queries, keys, values, bucket, w_out, grad_out):
    sources = lax.axis_size("seq")
    device = lax.axis_index("seq")
    token_rows = queries.shape[0]
    features = queries.shape[1]
    groups = features // HSZ
    slot_total = max(2, 3 * token_rows // (2 * sources))
    slot_rows = sources * slot_total
    scaling = 1.0 / math.sqrt(HSZ)
    bucket_grid = bucket[:, 0].reshape(sources, token_rows)
    back_index, send_index, send_live = local_slots(bucket_grid, device, sources, slot_total)
    where_here, alive_here = member_table(bucket_grid, device, slot_total)
    where_before, alive_before = member_table(bucket_grid, device - 1, slot_total)
    allowed = allowed_mask(where_here, alive_here, where_before, alive_before)
    grad_heads = lax.dot_general(
        grad_out, w_out, (((1,), (1,)), ((), ())), preferred_element_type=jnp.float32
    ).astype(jnp.bfloat16)

    def pack_rows(source):
        return jnp.take(source, send_index, axis=0) * send_live[:, None].astype(source.dtype)

    def split_heads(block):
        return block.reshape(block.shape[0], groups, HSZ)

    def flatten(block):
        return block.reshape(block.shape[0], features)

    query_rows, key_rows, value_rows = (
        lax.all_to_all(pack_rows(queries), "seq", split_axis=0, concat_axis=0, tiled=True),
        lax.all_to_all(pack_rows(keys), "seq", split_axis=0, concat_axis=0, tiled=True),
        lax.all_to_all(pack_rows(values), "seq", split_axis=0, concat_axis=0, tiled=True),
    )
    key_all, value_all = with_previous(key_rows, value_rows)
    probs = owner_probs(split_heads(query_rows), split_heads(key_all), allowed, scaling)
    rounded, attended = owner_forward(probs, split_heads(value_all))
    key_all, value_all, probs, rounded, attended = (key_all, value_all, probs, rounded, attended)
    returned = lax.all_to_all(flatten(attended), "seq", split_axis=0, concat_axis=0, tiled=True)
    grad_rows = lax.all_to_all(
        pack_rows(grad_heads), "seq", split_axis=0, concat_axis=0, tiled=True
    )
    grad_query, grad_key, grad_value = owner_backward(
        probs,
        rounded,
        attended,
        split_heads(grad_rows),
        split_heads(query_rows),
        split_heads(key_all),
        split_heads(value_all),
        scaling,
    )
    key_total, value_total = settle_keys(flatten(grad_key), flatten(grad_value), slot_rows)
    back_query, back_key, back_value = (
        lax.all_to_all(flatten(grad_query), "seq", split_axis=0, concat_axis=0, tiled=True),
        lax.all_to_all(key_total, "seq", split_axis=0, concat_axis=0, tiled=True),
        lax.all_to_all(value_total, "seq", split_axis=0, concat_axis=0, tiled=True),
    )
    attended_home = jnp.take(returned, back_index, axis=0)
    partial_value = jnp.dot(attended_home, w_out, preferred_element_type=jnp.float32)
    layer_out = lax.psum_scatter(
        partial_value.astype(jnp.bfloat16), "head", scatter_dimension=1, tiled=True
    )
    weight_terms = lax.dot_general(
        attended_home, grad_out, (((0,), (0,)), ((), ())), preferred_element_type=jnp.float32
    )
    grad_weight = lax.psum_scatter(weight_terms, "seq", scatter_dimension=1, tiled=True)
    grad_queries = jnp.take(back_query, back_index, axis=0)
    grad_keys = jnp.take(back_key, back_index, axis=0)
    grad_values = jnp.take(back_value, back_index, axis=0)
    return (layer_out, grad_queries, grad_keys, grad_values, grad_weight)


MESH = pl.DeviceIdType.MESH
NT = (((1,), (1,)), ((), ()))
TN = (((0,), (0,)), ((), ()))


def times(a, b, dims):
    return lax.dot_general(a, b, dims, preferred_element_type=jnp.float32)


def dense_kernel(
    seqs,
    heads,
    q_hbm,
    k_hbm,
    v_hbm,
    brow,
    w_hbm,
    go_hbm,
    lo_out,
    gq_out,
    gk_out,
    gv_out,
    gw_out,
    w_buf,
    go_buf,
    gh_buf,
    q_buf,
    g_buf,
    k_buf,
    v_buf,
    go_all,
    att_all,
    dq_send,
    dk_acc,
    dv_acc,
    dk_send,
    dv_send,
    dq_in,
    dk_in,
    dv_in,
    dk_far,
    dv_far,
    lo_send,
    lo_in,
    p_buf,
    local_sem,
    in_send,
    in_recv,
    far_send,
    far_recv,
    go_send,
    go_recv,
    gx_send,
    gx_recv,
    att_send,
    att_recv,
    fwd_send,
    fwd_recv,
    dq_ssem,
    dq_rsem,
    dk_ssem,
    dk_rsem,
    dkf_ssem,
    dkf_rsem,
    lo_ssem,
    lo_rsem,
):
    s = lax.axis_index("seq")
    h = lax.axis_index("head")
    rows = q_hbm.shape[0]
    width = HSZ
    groups = q_hbm.shape[1] // width
    half = lax.div(s, groups)
    mine = lax.rem(s, groups)
    part = groups * rows
    scaling = 1.0 / math.sqrt(HSZ)
    gcols = w_hbm.shape[1] // seqs
    lcols = w_hbm.shape[1] // heads
    quarter = rows // heads
    low = half == 0
    high = half == 1
    deep = lax.div(mine, 2)

    def flip(index, bits):
        out = index
        for bit in (1, 2, 4):
            if bits & bit:
                out = out + bit * (1 - 2 * lax.rem(lax.div(index, bit), 2))
        return out

    def near(r):
        return flip(mine, r)

    def rows_of(block):
        return pl.ds(pl.multiple_of(block * rows, rows), rows)

    def cols_of(block, size=width):
        return pl.ds(pl.multiple_of(block * size, size), size)

    def quarter_of(head):
        return pl.ds(pl.multiple_of(head * quarter, quarter), quarter)

    def remote(src, dst, ssem, rsem, where):
        return pltpu.make_async_remote_copy(
            src_ref=src, dst_ref=dst, send_sem=ssem, recv_sem=rsem, device_id=where,
            device_id_type=MESH,
        )

    x_to, z_to, d_to = (flip(s, 1), h), (flip(s, 2), h), (flip(s, 3), h)
    c_to = (flip(s, 4), h)
    core_to, y_to = (s, flip(h, 1)), (s, flip(h, 2))

    w_copy = pltpu.make_async_copy(w_hbm, w_buf, local_sem.at[0])
    go_copy = pltpu.make_async_copy(go_hbm, go_buf, local_sem.at[1])
    go_copy.start()
    w_copy.start()
    own = [
        pltpu.make_async_copy(k_hbm.at[:, cols_of(mine)], k_buf.at[rows_of(s), :], local_sem.at[2]),
        pltpu.make_async_copy(v_hbm.at[:, cols_of(mine)], v_buf.at[rows_of(s), :], local_sem.at[3]),
        pltpu.make_async_copy(q_hbm.at[:, cols_of(mine)], q_buf.at[rows_of(mine), :], local_sem.at[4]),
    ]
    for copy in own:
        copy.start()
    go_own = pltpu.make_async_copy(
        go_hbm.at[quarter_of(h), cols_of(s, gcols)], go_all.at[s, quarter_of(h), :], local_sem.at[5]
    )
    go_own.start()

    barrier = pltpu.get_barrier_semaphore()
    for r in range(1, seqs):
        pl.semaphore_signal(
            barrier, inc=1, device_id=(lax.rem(s + r, seqs), h), device_id_type=MESH
        )
    for there in (core_to, y_to):
        pl.semaphore_signal(barrier, inc=1, device_id=there, device_id_type=MESH)
    pl.semaphore_wait(barrier, seqs + 1)

    def cross_copies(sources, there_in, ssem, rsem):
        out = []
        for block in range(2):
            for side in range(2):
                to = 2 * block + lax.rem(mine + side, 2)
                for n, (src, dst) in enumerate(sources):
                    out.append(
                        remote(
                            src(to), dst, ssem.at[2 * block + side, n],
                            rsem.at[2 * deep + side, n], ((1 - half) * groups + to, there_in),
                        )
                    )
        return out

    def cross_arrivals(sources, ssem, rsem):
        return [
            remote(src(mine), dst, ssem.at[r, n], rsem.at[r, n], c_to)
            for r in range(groups)
            for n, (src, dst) in enumerate(sources)
        ]

    far_sources = (
        (lambda to: k_hbm.at[:, cols_of(to)], k_buf.at[rows_of(s), :]),
        (lambda to: v_hbm.at[:, cols_of(to)], v_buf.at[rows_of(s), :]),
    )
    far = cross_copies(far_sources, h, far_send, far_recv)
    far_in = cross_arrivals(far_sources, far_send, far_recv)

    @pl.when(low)
    def _():
        for copy in far[:4]:
            copy.start()

    inside = []
    for n, (src, dst, at) in enumerate(
        ((k_hbm, k_buf, s), (q_hbm, q_buf, mine), (v_hbm, v_buf, s))
    ):
        for r in (3, 2, 1):
            to = near(r)
            copy = remote(
                src.at[:, cols_of(to)], dst.at[rows_of(at), :], in_send.at[r, n],
                in_recv.at[r, n], (half * groups + to, h),
            )
            copy.start()
            inside.append(copy)
    spread = []
    for r in range(1, seqs):
        to = lax.rem(s + r, seqs)
        spread.append(
            remote(
                go_hbm.at[quarter_of(h), cols_of(to, gcols)], go_all.at[s, quarter_of(h), :],
                go_send.at[r], go_recv.at[s], (to, h),
            )
        )
    spread_in = [
        remote(
            go_hbm.at[quarter_of(h), cols_of(s, gcols)], go_all.at[source, quarter_of(h), :],
            go_send.at[0], go_recv.at[source], x_to,
        )
        for source in range(seqs)
    ]

    @pl.when(low)
    def _():
        for copy in far[4:]:
            copy.start()

    @pl.when(high)
    def _():
        for copy in spread:
            copy.start()

    @pl.when(low)
    def _():
        k_buf[pl.ds(part, part), :] = jnp.zeros((part, width), k_buf.dtype)
        v_buf[pl.ds(part, part), :] = jnp.zeros((part, width), v_buf.dtype)

    @pl.when(high)
    def _():
        dk_far[...] = jnp.zeros_like(dk_far)
        dv_far[...] = jnp.zeros_like(dv_far)

    go_copy.wait()
    w_copy.wait()
    depth = w_buf.shape[1] // seqs

    def heads_step(c, total):
        at = pl.ds(pl.multiple_of(c * depth, depth), depth)
        return total + times(go_buf[:, at], w_buf[:, at], NT)

    gh = lax.fori_loop(
        0, seqs, heads_step, jnp.zeros((rows, groups * width), jnp.float32)
    )
    gh_buf[...] = gh.astype(jnp.bfloat16)
    gh_near = []
    for r in (3, 2, 1):
        to = near(r)
        copy = remote(
            gh_buf.at[:, cols_of(to)], g_buf.at[rows_of(mine), :], in_send.at[r, 3],
            in_recv.at[r, 3], (half * groups + to, h),
        )
        copy.start()
        gh_near.append(copy)
    g_buf[rows_of(mine), :] = gh_buf[:, cols_of(mine)]

    @pl.when(low)
    def _():
        for copy in spread:
            copy.start()

    for copy in own:
        copy.wait()
    for copy in inside:
        copy.wait_recv()

    @pl.when(high)
    def _():
        for copy in far_in:
            copy.wait_recv()

    def piece(token, head, kind, there):
        at = att_all.at[rows_of(token), cols_of(head)]
        lane, step = kind
        return remote(at, at, att_send.at[lane, step], att_recv.at[lane, step], there)

    def onward(token, head, kind, there):
        at = att_all.at[rows_of(token), cols_of(head)]
        lane, step = kind
        return remote(at, at, fwd_send.at[lane, step], fwd_recv.at[lane, step], there)

    keys_bucket = brow[...].astype(jnp.float32)
    diagonal = lax.broadcasted_iota(jnp.int32, (rows, rows), 0) == lax.broadcasted_iota(
        jnp.int32, (rows, rows), 1
    )
    keys_at = lax.broadcasted_iota(jnp.int32, (rows, seqs * rows), 1)
    order = (3, 1, 2, 0)
    def go_part(first, head, index, where):
        at = go_all.at[pl.ds(first, groups), quarter_of(head), :]
        return remote(at, at, gx_send.at[index], gx_recv.at[index], where)

    go_moves = [
        [
            go_part(first, h, 3 * n, y_to),
            go_part(first, h, 3 * n + 1, core_to),
            go_part(first, flip(h, 2), 3 * n + 2, core_to),
        ]
        for n, first in enumerate((groups, 0))
    ]

    def go_exchange(n):
        first = (groups, 0)[n]

        @pl.when(half == 1 - n)
        def _():
            go_own.wait()

        for source in range(first, first + groups):

            @pl.when(s != source)
            def _():
                spread_in[source].wait_recv()

        go_moves[n][0].start()
        go_moves[n][1].start()

    att_x, att_z, att_c, att_d = {}, {}, {}, {}
    dq_near = []
    for step, r in enumerate(order):
        block = near(r)
        token = half * groups + block
        qc = q_buf[rows_of(block), :]
        k_all = k_buf[...]
        v_all = v_buf[...]
        along = brow[:, cols_of(token, rows)].astype(jnp.float32)
        gap = jnp.sum(jnp.where(diagonal, along, 0.0), axis=1, keepdims=True) - keys_bucket
        query_at = token * rows + lax.broadcasted_iota(jnp.int32, (rows, seqs * rows), 0)
        allowed = ((gap == 0.0) | (gap == 1.0)) & (keys_at <= query_at)
        scores = jnp.where(allowed, times(qc, k_all, NT) * scaling, -1e30)
        largest = jnp.max(scores, axis=1, keepdims=True)
        weights = jnp.where(allowed, jnp.exp(scores - largest), 0.0)
        probs = weights * (1.0 / jnp.sum(weights, axis=1, keepdims=True))
        p_buf[step] = probs
        attended = jnp.dot(
            probs.astype(jnp.bfloat16), v_all, preferred_element_type=jnp.float32
        ).astype(jnp.bfloat16)
        att_all[rows_of(token), cols_of(mine)] = attended
        if r == 3:
            att_d[r] = piece(token, mine, (3, step), d_to)
            att_d[r].start()
        att_c[r] = piece(token, mine, (2, step), c_to)
        att_z[r] = piece(token, mine, (1, step), z_to)
        att_x[r] = piece(token, mine, (0, step), x_to)
        for copy in (att_z[r], att_x[r], att_c[r]):
            copy.start()

    cross_z, cross_x = {}, {}
    for step, r in enumerate(order):
        token = (1 - half) * groups + near(r)
        cross_z[r] = onward(token, mine, (1, step), z_to)
        cross_x[r] = onward(token, mine, (2, step), x_to)

    def pass_cross():
        for r in order:
            att_c[r].wait_recv()
            cross_z[r].start()
            cross_x[r].start()

    go_exchange(0)

    @pl.when(low)
    def _():
        go_exchange(1)

    for copy in gh_near:
        copy.wait_recv()
    for step, r in enumerate(order):
        block = near(r)
        token = half * groups + block
        qc = q_buf[rows_of(block), :]
        gc = g_buf[rows_of(block), :]
        k_all = k_buf[...]
        v_all = v_buf[...]
        probs = p_buf[step]
        rounded = probs.astype(jnp.bfloat16)
        attended = att_all[rows_of(token), cols_of(mine)]
        centre = jnp.sum(
            attended.astype(jnp.float32) * gc.astype(jnp.float32), axis=1, keepdims=True
        )
        dscores = (probs * (times(gc, v_all, NT) - centre)).astype(jnp.bfloat16)
        dq = (jnp.dot(dscores, k_all, preferred_element_type=jnp.float32) * scaling).astype(
            jnp.bfloat16
        )
        if r == 0:
            dq_in[:, cols_of(mine)] = dq
        else:
            dq_send[r] = dq
            copy = remote(
                dq_send.at[r], dq_in.at[:, cols_of(mine)], dq_ssem.at[r], dq_rsem.at[r],
                (token, h),
            )
            copy.start()
            dq_near.append(copy)
        dk = times(dscores, qc, TN)
        dv = times(rounded, gc, TN)
        if step == 0:
            dk_acc[...] = dk
            dv_acc[...] = dv
        else:
            dk_acc[...] += dk
            dv_acc[...] += dv

    dk_send[...] = (dk_acc[...] * scaling).astype(jnp.bfloat16)
    dv_send[...] = dv_acc[...].astype(jnp.bfloat16)
    dk_sources = (
        (lambda to: dk_send.at[rows_of(to), :], dk_far.at[:, cols_of(mine)]),
        (lambda to: dv_send.at[rows_of(to), :], dv_far.at[:, cols_of(mine)]),
    )
    dk_cross = cross_copies(dk_sources, h, dkf_ssem, dkf_rsem)
    dk_cross_in = cross_arrivals(dk_sources, dkf_ssem, dkf_rsem)

    @pl.when(high)
    def _():
        for copy in dk_cross:
            copy.start()

    dk_near = []
    for r in range(1, groups):
        to = near(r)
        for n, (src, dst) in enumerate(((dk_send, dk_in), (dv_send, dv_in))):
            copy = remote(
                src.at[rows_of(half * groups + to), :], dst.at[:, cols_of(mine)],
                dk_ssem.at[r, n], dk_rsem.at[r, n], (half * groups + to, h),
            )
            copy.start()
            dk_near.append(copy)
    dk_in[:, cols_of(mine)] = dk_send[rows_of(s), :]
    dv_in[:, cols_of(mine)] = dv_send[rows_of(s), :]

    def own_token(bits):
        return half * groups + near(bits)

    def other_token(bits):
        return (1 - half) * groups + near(bits)


    @pl.when(high)
    def _():
        go_exchange(1)


    @pl.when(high)
    def _():
        pass_cross()

    fwd_near = {}
    for step, r in enumerate(order):
        if r != 3:
            fwd_near[r] = onward(own_token(2 ^ r), near(2), (0, step), x_to)
            att_z[r].wait_recv()
            fwd_near[r].start()
    go_moves[0][0].wait_recv()
    go_moves[0][2].start()

    @pl.when(low)
    def _():
        go_moves[1][0].wait_recv()
        go_moves[1][2].start()


    att_x[1].wait_recv()
    att_d[3].wait_recv()
    home = att_all[rows_of(s), :]

    def partial_for(head):
        return jnp.dot(home, w_buf[:, cols_of(head, lcols)], preferred_element_type=jnp.float32)

    lo_moves = [
        remote(lo_send.at[0], lo_in.at[0], lo_ssem.at[0], lo_rsem.at[0], core_to),
        remote(lo_send.at[1], lo_in.at[1], lo_ssem.at[1], lo_rsem.at[1], core_to),
        remote(lo_send.at[2], lo_in.at[2], lo_ssem.at[2], lo_rsem.at[2], y_to),
    ]
    lo_send[0] = partial_for(flip(h, 3)).astype(jnp.bfloat16)
    lo_moves[0].start()
    across = partial_for(flip(h, 2))
    lo_moves[0].wait_recv()
    lo_send[2] = (across + lo_in[0].astype(jnp.float32)).astype(jnp.bfloat16)
    lo_moves[2].start()
    lo_send[1] = partial_for(flip(h, 1)).astype(jnp.bfloat16)
    lo_moves[1].start()
    layer = partial_for(h)


    @pl.when(low)
    def _():
        pass_cross()


    @pl.when(high)
    def _():
        go_moves[1][0].wait_recv()
        go_moves[1][2].start()

    cross_on = {}
    for step, r in enumerate(order):
        cross_on[r] = onward(other_token(2 ^ r), near(2), (3, step), x_to)
        cross_z[r].wait_recv()
        cross_on[r].start()

    def weight_rows(bits):
        head = near(bits)
        gw_out[rows_of(head), :] = times(
            att_all[:, cols_of(head)], go_all[...].reshape(seqs * rows, gcols), TN
        )

    for n in range(2):
        go_moves[n][1].wait_recv()
        go_moves[n][2].wait_recv()
    weight_rows(0)
    att_z[3].wait_recv()
    weight_rows(2)
    for copy in dq_near:
        copy.wait_recv()
    gq_out[...] = dq_in[...]
    lo_moves[1].wait_recv()
    lo_moves[2].wait_recv()
    lo_out[...] = (layer + lo_in[1].astype(jnp.float32) + lo_in[2].astype(jnp.float32)).astype(
        jnp.bfloat16
    )
    for r in order:
        if r != 1:
            att_x[r].wait_recv()
        cross_x[r].wait_recv()
    weight_rows(1)
    for copy in dk_near:
        copy.wait_recv()

    @pl.when(low)
    def _():
        for copy in dk_cross_in:
            copy.wait_recv()

    gk_out[...] = (dk_in[...].astype(jnp.float32) + dk_far[...].astype(jnp.float32)).astype(
        jnp.bfloat16
    )
    gv_out[...] = (dv_in[...].astype(jnp.float32) + dv_far[...].astype(jnp.float32)).astype(
        jnp.bfloat16
    )
    for r in order:
        if r != 3:
            fwd_near[r].wait_recv()
        cross_on[r].wait_recv()
    weight_rows(3)

    moved = inside + gh_near + spread + go_moves[0] + go_moves[1] + dq_near + dk_near + lo_moves
    for group in (att_x, att_z, att_c, att_d, fwd_near, cross_z, cross_x, cross_on):
        moved += list(group.values())
    for copy in moved:
        copy.wait_send()

    @pl.when(low)
    def _():
        for copy in far:
            copy.wait_send()

    @pl.when(high)
    def _():
        for copy in dk_cross:
            copy.wait_send()


def place_kernel(*refs):
    sem = refs[-1]
    half = len(refs) // 2
    copies = [
        pltpu.make_async_copy(refs[n], refs[half + n], sem.at[n]) for n in range(half)
    ]
    for copy in copies:
        copy.start()
    for copy in copies:
        copy.wait()


def dense_device(queries, keys, values, bucket, w_out, grad_out):
    seqs = lax.axis_size("seq")
    heads = lax.axis_size("head")
    rows, features = queries.shape
    model = w_out.shape[1]
    groups = features // HSZ
    part = groups * rows
    tokens = seqs * rows
    bf, f32 = jnp.bfloat16, jnp.float32
    vmem = pl.BlockSpec(memory_space=pltpu.VMEM)
    hbm = pl.BlockSpec(memory_space=pl.ANY)
    dma = pltpu.SemaphoreType.DMA
    wide = pltpu.VMEM((rows, features), bf)
    sems = []
    for shape in (
        (groups, 4), (groups, 2), (seqs,), (6,), (4, groups), (4, groups), (groups,), (groups, 2),
        (groups, 2), (3,),
    ):
        sems += [dma(shape), dma(shape)]
    shapes = (
        ((rows, model // heads), bf),
        ((rows, features), bf),
        ((rows, features), bf),
        ((rows, features), bf),
        ((features, model // seqs), f32),
    )
    made = pl.pallas_call(
        functools.partial(dense_kernel, seqs, heads),
        out_shape=tuple(pltpu.VMEM(shape, dtype) for shape, dtype in shapes),
        in_specs=[hbm, hbm, hbm, vmem, hbm, hbm],
        out_specs=(vmem,) * 5,
        scratch_shapes=[
            pltpu.VMEM(w_out.shape, bf),
            pltpu.VMEM(grad_out.shape, bf),
            wide,
            pltpu.VMEM((part, HSZ), bf),
            pltpu.VMEM((part, HSZ), bf),
            pltpu.VMEM((tokens, HSZ), bf),
            pltpu.VMEM((tokens, HSZ), bf),
            pltpu.VMEM((seqs, rows, model // seqs), bf),
            pltpu.VMEM((tokens, features), bf),
            pltpu.VMEM((groups, rows, HSZ), bf),
            pltpu.VMEM((tokens, HSZ), f32),
            pltpu.VMEM((tokens, HSZ), f32),
            pltpu.VMEM((tokens, HSZ), bf),
            pltpu.VMEM((tokens, HSZ), bf),
            wide,
            wide,
            wide,
            wide,
            wide,
            pltpu.VMEM((3, rows, model // heads), bf),
            pltpu.VMEM((3, rows, model // heads), bf),
            pltpu.VMEM((groups, rows, tokens), f32),
            dma((6,)),
        ]
        + sems,
        compiler_params=pltpu.CompilerParams(
            collective_id=0, has_side_effects=True, vmem_limit_bytes=58 * 2**20
        ),
    )(queries, keys, values, bucket.reshape(1, -1), w_out, grad_out)
    return pl.pallas_call(
        place_kernel,
        out_shape=tuple(jax.ShapeDtypeStruct(shape, dtype) for shape, dtype in shapes),
        in_specs=[vmem] * 5,
        out_specs=(hbm,) * 5,
        scratch_shapes=[dma((5,))],
    )(*[pltpu.with_memory_space_constraint(one, pltpu.VMEM) for one in made])


def choose(queries, keys, values, bucket, w_out, grad_out):
    groups = queries.shape[1] // HSZ
    dense = groups == 4 and lax.axis_size("seq") == 8 and lax.axis_size("head") == 4
    plan = dense_device if dense else per_device
    return plan(queries, keys, values, bucket, w_out, grad_out)


def solution(mesh):
    return jax.shard_map(
        choose,
        mesh=mesh,
        in_specs=(
            P("seq", "head"),
            P("seq", "head"),
            P("seq", "head"),
            P(),
            P("head", None),
            P("seq", None),
        ),
        out_specs=(
            P("seq", "head"),
            P("seq", "head"),
            P("seq", "head"),
            P("seq", "head"),
            P("head", "seq"),
        ),
        check_vma=False,
    )
```

```python
import functools
import math

import jax
import jax.numpy as jnp
from jax import lax
from jax.experimental import pallas as pl
from jax.experimental.pallas import tpu as pltpu
from jax.sharding import PartitionSpec as P

HSZ = 128


def passed_along(value, axis, by):
    length = lax.axis_size(axis)
    pairs = [(i, i + by) for i in range(length) if 0 <= i + by < length]
    return lax.ppermute(value, axis, pairs)


def earlier_count(flags, axis):
    length = flags.shape[axis]
    at = jnp.arange(length)
    if axis == 0:
        before = (at[None, :] < at[:, None]).astype(jnp.float32)
        return jnp.dot(before, flags.astype(jnp.float32)).astype(jnp.int32)
    before = (at[:, None] < at[None, :]).astype(jnp.float32)
    return jnp.dot(flags.astype(jnp.float32), before).astype(jnp.int32)


def member_table(bucket_grid, owner, slot_count):
    matches = (bucket_grid == owner).astype(jnp.int32)
    ranking = earlier_count(matches, 1)
    slot_ids = jnp.arange(slot_count, dtype=jnp.int32)
    placed = matches[:, :, None] * (ranking[:, :, None] == slot_ids[None, None, :]).astype(
        jnp.int32
    )
    sources = bucket_grid.shape[0]
    stride = bucket_grid.shape[1]
    offsets = (
        jnp.arange(sources, dtype=jnp.int32)[:, None] * stride
        + jnp.arange(stride, dtype=jnp.int32)[None, :]
    )
    where_at = jnp.sum(placed * offsets[:, :, None], axis=1).reshape(-1)
    present = jnp.sum(placed, axis=1).reshape(-1)
    return (where_at, present)


def allowed_mask(where_here, alive_here, where_before, alive_before):
    amount = where_here.shape[0]
    asking = alive_here[:, None] > 0
    inside = (where_here[None, :] <= where_here[:, None]) & (alive_here[None, :] > 0) & asking
    inside = inside | (jnp.arange(amount)[:, None] == jnp.arange(amount)[None, :])
    earlier = (where_before[None, :] <= where_here[:, None]) & (alive_before[None, :] > 0) & asking
    return jnp.concatenate([inside, earlier], axis=1)


def softmax_rows(scores, allowed):
    masked = jnp.where(allowed[None], scores, -1e30)
    largest = jnp.max(masked, axis=2, keepdims=True)
    weights = jnp.where(allowed[None], jnp.exp(masked - largest), 0.0)
    return weights / jnp.sum(weights, axis=2, keepdims=True)


def local_slots(bucket_grid, device, sources, slot_total):
    my_buckets = lax.dynamic_index_in_dim(bucket_grid, device, 0, keepdims=False)
    owners = jnp.arange(sources, dtype=jnp.int32)
    onehot = (my_buckets[:, None] == owners[None, :]).astype(jnp.int32)
    ranking = jnp.sum(earlier_count(onehot, 0) * onehot, axis=1)
    back_index = my_buckets * slot_total + ranking
    slot_ids = jnp.arange(slot_total, dtype=jnp.int32)
    placed = onehot[:, :, None] * (ranking[:, None, None] == slot_ids[None, None, :]).astype(
        jnp.int32
    )
    token_ids = jnp.arange(my_buckets.shape[0], dtype=jnp.int32)
    send_index = jnp.sum(placed * token_ids[:, None, None], axis=0).reshape(-1)
    send_live = jnp.sum(placed, axis=0).reshape(-1)
    return (back_index, send_index, send_live)


def owner_probs(query_rows, key_all, allowed, scaling):
    scores = (
        jnp.einsum("qgd,kgd->gqk", query_rows, key_all, preferred_element_type=jnp.float32)
        * scaling
    )
    return softmax_rows(scores, allowed)


def owner_forward(probs, value_all):
    rounded = probs.astype(jnp.bfloat16)
    attended = jnp.einsum(
        "gqk,kgd->qgd", rounded, value_all, preferred_element_type=jnp.float32
    ).astype(jnp.bfloat16)
    return (rounded, attended)


def owner_backward(probs, rounded, attended, grad_rows, query_rows, key_all, value_all, scaling):
    centre = jnp.sum(attended.astype(jnp.float32) * grad_rows.astype(jnp.float32), axis=2)
    dprobs = jnp.einsum("qgd,kgd->gqk", grad_rows, value_all, preferred_element_type=jnp.float32)
    dscores = probs * (dprobs - jnp.transpose(centre)[:, :, None])
    dround = dscores.astype(jnp.bfloat16)
    grad_query = (
        jnp.einsum("gqk,kgd->qgd", dround, key_all, preferred_element_type=jnp.float32) * scaling
    ).astype(jnp.bfloat16)
    grad_key = (
        jnp.einsum("gqk,qgd->kgd", dround, query_rows, preferred_element_type=jnp.float32) * scaling
    )
    grad_value = jnp.einsum("gqk,qgd->kgd", rounded, grad_rows, preferred_element_type=jnp.float32)
    return (grad_query, grad_key, grad_value)


def with_previous(key_rows, value_rows):
    key_before, value_before = passed_along((key_rows, value_rows), "seq", 1)
    return (
        jnp.concatenate([key_rows, key_before], axis=0),
        jnp.concatenate([value_rows, value_before], axis=0),
    )


def settle_keys(grad_key, grad_value, slot_rows):
    key_next, value_next = passed_along(
        (grad_key[slot_rows:].astype(jnp.bfloat16), grad_value[slot_rows:].astype(jnp.bfloat16)),
        "seq",
        -1,
    )
    key_total = (grad_key[:slot_rows] + key_next.astype(jnp.float32)).astype(jnp.bfloat16)
    value_total = (grad_value[:slot_rows] + value_next.astype(jnp.float32)).astype(jnp.bfloat16)
    return (key_total, value_total)


def per_device(queries, keys, values, bucket, w_out, grad_out):
    sources = lax.axis_size("seq")
    device = lax.axis_index("seq")
    token_rows = queries.shape[0]
    features = queries.shape[1]
    groups = features // HSZ
    slot_total = max(2, 3 * token_rows // (2 * sources))
    slot_rows = sources * slot_total
    scaling = 1.0 / math.sqrt(HSZ)
    bucket_grid = bucket[:, 0].reshape(sources, token_rows)
    back_index, send_index, send_live = local_slots(bucket_grid, device, sources, slot_total)
    where_here, alive_here = member_table(bucket_grid, device, slot_total)
    where_before, alive_before = member_table(bucket_grid, device - 1, slot_total)
    allowed = allowed_mask(where_here, alive_here, where_before, alive_before)
    grad_heads = lax.dot_general(
        grad_out, w_out, (((1,), (1,)), ((), ())), preferred_element_type=jnp.float32
    ).astype(jnp.bfloat16)

    def pack_rows(source):
        return jnp.take(source, send_index, axis=0) * send_live[:, None].astype(source.dtype)

    def split_heads(block):
        return block.reshape(block.shape[0], groups, HSZ)

    def flatten(block):
        return block.reshape(block.shape[0], features)

    query_rows, key_rows, value_rows = (
        lax.all_to_all(pack_rows(queries), "seq", split_axis=0, concat_axis=0, tiled=True),
        lax.all_to_all(pack_rows(keys), "seq", split_axis=0, concat_axis=0, tiled=True),
        lax.all_to_all(pack_rows(values), "seq", split_axis=0, concat_axis=0, tiled=True),
    )
    key_all, value_all = with_previous(key_rows, value_rows)
    probs = owner_probs(split_heads(query_rows), split_heads(key_all), allowed, scaling)
    rounded, attended = owner_forward(probs, split_heads(value_all))
    key_all, value_all, probs, rounded, attended = (key_all, value_all, probs, rounded, attended)
    returned = lax.all_to_all(flatten(attended), "seq", split_axis=0, concat_axis=0, tiled=True)
    grad_rows = lax.all_to_all(
        pack_rows(grad_heads), "seq", split_axis=0, concat_axis=0, tiled=True
    )
    grad_query, grad_key, grad_value = owner_backward(
        probs,
        rounded,
        attended,
        split_heads(grad_rows),
        split_heads(query_rows),
        split_heads(key_all),
        split_heads(value_all),
        scaling,
    )
    key_total, value_total = settle_keys(flatten(grad_key), flatten(grad_value), slot_rows)
    back_query, back_key, back_value = (
        lax.all_to_all(flatten(grad_query), "seq", split_axis=0, concat_axis=0, tiled=True),
        lax.all_to_all(key_total, "seq", split_axis=0, concat_axis=0, tiled=True),
        lax.all_to_all(value_total, "seq", split_axis=0, concat_axis=0, tiled=True),
    )
    attended_home = jnp.take(returned, back_index, axis=0)
    partial_value = jnp.dot(attended_home, w_out, preferred_element_type=jnp.float32)
    layer_out = lax.psum_scatter(
        partial_value.astype(jnp.bfloat16), "head", scatter_dimension=1, tiled=True
    )
    weight_terms = lax.dot_general(
        attended_home, grad_out, (((0,), (0,)), ((), ())), preferred_element_type=jnp.float32
    )
    grad_weight = lax.psum_scatter(weight_terms, "seq", scatter_dimension=1, tiled=True)
    grad_queries = jnp.take(back_query, back_index, axis=0)
    grad_keys = jnp.take(back_key, back_index, axis=0)
    grad_values = jnp.take(back_value, back_index, axis=0)
    return (layer_out, grad_queries, grad_keys, grad_values, grad_weight)


MESH = pl.DeviceIdType.MESH
NT = (((1,), (1,)), ((), ()))
TN = (((0,), (0,)), ((), ()))


def times(a, b, dims):
    return lax.dot_general(a, b, dims, preferred_element_type=jnp.float32)


def dense_kernel(
    seqs,
    heads,
    q_hbm,
    k_hbm,
    v_hbm,
    brow,
    w_hbm,
    go_hbm,
    lo_out,
    gq_out,
    gk_out,
    gv_out,
    gw_out,
    w_buf,
    go_buf,
    gh_buf,
    q_buf,
    g_buf,
    k_buf,
    v_buf,
    go_all,
    att_all,
    dq_send,
    dk_acc,
    dv_acc,
    dk_send,
    dv_send,
    dq_in,
    dk_in,
    dv_in,
    dk_far,
    dv_far,
    lo_send,
    lo_in,
    p_buf,
    local_sem,
    in_send,
    in_recv,
    far_send,
    far_recv,
    go_send,
    go_recv,
    gx_send,
    gx_recv,
    att_send,
    att_recv,
    fwd_send,
    fwd_recv,
    dq_ssem,
    dq_rsem,
    dk_ssem,
    dk_rsem,
    dkf_ssem,
    dkf_rsem,
    lo_ssem,
    lo_rsem,
):
    s = lax.axis_index("seq")
    h = lax.axis_index("head")
    rows = q_hbm.shape[0]
    width = HSZ
    groups = q_hbm.shape[1] // width
    half = lax.div(s, groups)
    mine = lax.rem(s, groups)
    part = groups * rows
    scaling = 1.0 / math.sqrt(HSZ)
    gcols = w_hbm.shape[1] // seqs
    lcols = w_hbm.shape[1] // heads
    quarter = rows // heads
    low = half == 0
    high = half == 1
    deep = lax.div(mine, 2)

    def flip(index, bits):
        out = index
        for bit in (1, 2, 4):
            if bits & bit:
                out = out + bit * (1 - 2 * lax.rem(lax.div(index, bit), 2))
        return out

    def near(r):
        return flip(mine, r)

    def rows_of(block):
        return pl.ds(pl.multiple_of(block * rows, rows), rows)

    def cols_of(block, size=width):
        return pl.ds(pl.multiple_of(block * size, size), size)

    def quarter_of(head):
        return pl.ds(pl.multiple_of(head * quarter, quarter), quarter)

    def remote(src, dst, ssem, rsem, where):
        return pltpu.make_async_remote_copy(
            src_ref=src, dst_ref=dst, send_sem=ssem, recv_sem=rsem, device_id=where,
            device_id_type=MESH,
        )

    x_to, z_to, d_to = (flip(s, 1), h), (flip(s, 2), h), (flip(s, 3), h)
    c_to, across_to = (flip(s, 4), h), (s + 2 - 4 * half, h)
    core_to, y_to = (s, flip(h, 1)), (s, flip(h, 2))

    w_copy = pltpu.make_async_copy(w_hbm, w_buf, local_sem.at[0])
    go_copy = pltpu.make_async_copy(go_hbm, go_buf, local_sem.at[1])
    go_copy.start()
    w_copy.start()
    own = [
        pltpu.make_async_copy(k_hbm.at[:, cols_of(mine)], k_buf.at[rows_of(s), :], local_sem.at[2]),
        pltpu.make_async_copy(v_hbm.at[:, cols_of(mine)], v_buf.at[rows_of(s), :], local_sem.at[3]),
        pltpu.make_async_copy(q_hbm.at[:, cols_of(mine)], q_buf.at[rows_of(mine), :], local_sem.at[4]),
    ]
    for copy in own:
        copy.start()
    go_own = pltpu.make_async_copy(
        go_hbm.at[quarter_of(h), cols_of(s, gcols)], go_all.at[s, quarter_of(h), :], local_sem.at[5]
    )
    go_own.start()

    barrier = pltpu.get_barrier_semaphore()
    for r in range(1, seqs):
        pl.semaphore_signal(
            barrier, inc=1, device_id=(lax.rem(s + r, seqs), h), device_id_type=MESH
        )
    for there in (core_to, y_to):
        pl.semaphore_signal(barrier, inc=1, device_id=there, device_id_type=MESH)
    pl.semaphore_wait(barrier, seqs + 1)

    def cross_copies(sources, there_in, ssem, rsem):
        out = []
        for block in range(2):
            for side in range(2):
                to = 2 * block + lax.rem(mine + side, 2)
                for n, (src, dst) in enumerate(sources):
                    out.append(
                        remote(
                            src(to), dst, ssem.at[2 * block + side, n],
                            rsem.at[2 * deep + side, n], ((1 - half) * groups + to, there_in),
                        )
                    )
        return out

    def cross_arrivals(sources, ssem, rsem):
        return [
            remote(src(mine), dst, ssem.at[r, n], rsem.at[r, n], c_to)
            for r in range(groups)
            for n, (src, dst) in enumerate(sources)
        ]

    far_sources = (
        (lambda to: k_hbm.at[:, cols_of(to)], k_buf.at[rows_of(s), :]),
        (lambda to: v_hbm.at[:, cols_of(to)], v_buf.at[rows_of(s), :]),
    )
    far = cross_copies(far_sources, h, far_send, far_recv)
    far_in = cross_arrivals(far_sources, far_send, far_recv)

    @pl.when(low)
    def _():
        for copy in far[:4]:
            copy.start()

    inside = []
    for n, (src, dst, at) in enumerate(
        ((k_hbm, k_buf, s), (q_hbm, q_buf, mine), (v_hbm, v_buf, s))
    ):
        for r in (3, 2, 1):
            to = near(r)
            copy = remote(
                src.at[:, cols_of(to)], dst.at[rows_of(at), :], in_send.at[r, n],
                in_recv.at[r, n], (half * groups + to, h),
            )
            copy.start()
            inside.append(copy)
    spread = []
    for r in range(1, seqs):
        to = lax.rem(s + r, seqs)
        spread.append(
            remote(
                go_hbm.at[quarter_of(h), cols_of(to, gcols)], go_all.at[s, quarter_of(h), :],
                go_send.at[r], go_recv.at[s], (to, h),
            )
        )
    spread_in = [
        remote(
            go_hbm.at[quarter_of(h), cols_of(s, gcols)], go_all.at[source, quarter_of(h), :],
            go_send.at[0], go_recv.at[source], x_to,
        )
        for source in range(seqs)
    ]

    @pl.when(low)
    def _():
        for copy in far[4:]:
            copy.start()

    @pl.when(high)
    def _():
        for copy in spread:
            copy.start()

    @pl.when(low)
    def _():
        k_buf[pl.ds(part, part), :] = jnp.zeros((part, width), k_buf.dtype)
        v_buf[pl.ds(part, part), :] = jnp.zeros((part, width), v_buf.dtype)

    @pl.when(high)
    def _():
        dk_far[...] = jnp.zeros_like(dk_far)
        dv_far[...] = jnp.zeros_like(dv_far)

    go_copy.wait()
    w_copy.wait()
    depth = w_buf.shape[1] // seqs

    def heads_step(c, total):
        at = pl.ds(pl.multiple_of(c * depth, depth), depth)
        return total + times(go_buf[:, at], w_buf[:, at], NT)

    gh = lax.fori_loop(
        0, seqs, heads_step, jnp.zeros((rows, groups * width), jnp.float32)
    )
    gh_buf[...] = gh.astype(jnp.bfloat16)
    gh_near = []
    for r in (3, 2, 1):
        to = near(r)
        copy = remote(
            gh_buf.at[:, cols_of(to)], g_buf.at[rows_of(mine), :], in_send.at[r, 3],
            in_recv.at[r, 3], (half * groups + to, h),
        )
        copy.start()
        gh_near.append(copy)
    g_buf[rows_of(mine), :] = gh_buf[:, cols_of(mine)]

    @pl.when(low)
    def _():
        for copy in spread:
            copy.start()

    for copy in own:
        copy.wait()
    for copy in inside:
        copy.wait_recv()

    @pl.when(high)
    def _():
        for copy in far_in:
            copy.wait_recv()

    def piece(token, head, kind, there):
        at = att_all.at[rows_of(token), cols_of(head)]
        lane, step = kind
        return remote(at, at, att_send.at[lane, step], att_recv.at[lane, step], there)

    def onward(token, head, out, into, step, there):
        at = att_all.at[rows_of(token), cols_of(head)]
        return remote(at, at, fwd_send.at[out, step], fwd_recv.at[into, step], there)

    def own_token(bits):
        return half * groups + near(bits)

    def other_token(bits):
        return (1 - half) * groups + near(bits)

    keys_bucket = brow[...].astype(jnp.float32)
    diagonal = lax.broadcasted_iota(jnp.int32, (rows, rows), 0) == lax.broadcasted_iota(
        jnp.int32, (rows, rows), 1
    )
    keys_at = lax.broadcasted_iota(jnp.int32, (rows, seqs * rows), 1)
    order = (3, 1, 2, 0)
    def go_part(first, head, index, where):
        at = go_all.at[pl.ds(first, groups), quarter_of(head), :]
        return remote(at, at, gx_send.at[index], gx_recv.at[index], where)

    go_moves = [
        [
            go_part(first, h, 3 * n, y_to),
            go_part(first, h, 3 * n + 1, core_to),
            go_part(first, flip(h, 2), 3 * n + 2, core_to),
        ]
        for n, first in enumerate((groups, 0))
    ]

    def go_exchange(n):
        first = (groups, 0)[n]

        @pl.when(half == 1 - n)
        def _():
            go_own.wait()

        for source in range(first, first + groups):

            @pl.when(s != source)
            def _():
                spread_in[source].wait_recv()

        go_moves[n][0].start()
        go_moves[n][1].start()

    att_x, att_z, att_c, att_h, att_d = {}, {}, {}, {}, {}
    dq_near = []
    for step, r in enumerate(order):
        block = near(r)
        token = half * groups + block
        qc = q_buf[rows_of(block), :]
        k_all = k_buf[...]
        v_all = v_buf[...]
        along = brow[:, cols_of(token, rows)].astype(jnp.float32)
        gap = jnp.sum(jnp.where(diagonal, along, 0.0), axis=1, keepdims=True) - keys_bucket
        query_at = token * rows + lax.broadcasted_iota(jnp.int32, (rows, seqs * rows), 0)
        allowed = ((gap == 0.0) | (gap == 1.0)) & (keys_at <= query_at)
        scores = jnp.where(allowed, times(qc, k_all, NT) * scaling, -1e30)
        largest = jnp.max(scores, axis=1, keepdims=True)
        weights = jnp.where(allowed, jnp.exp(scores - largest), 0.0)
        probs = weights * (1.0 / jnp.sum(weights, axis=1, keepdims=True))
        p_buf[step] = probs
        attended = jnp.dot(
            probs.astype(jnp.bfloat16), v_all, preferred_element_type=jnp.float32
        ).astype(jnp.bfloat16)
        att_all[rows_of(token), cols_of(mine)] = attended
        if r == 3:
            att_d[r] = piece(token, mine, (3, step), d_to)
            att_d[r].start()
        att_c[r] = onward(token, mine, 1, 1, step, across_to)
        att_h[r] = onward(token, mine, 1, 0, step, c_to)
        att_z[r] = piece(token, mine, (1, step), z_to)
        att_x[r] = piece(token, mine, (0, step), x_to)
        for copy in (att_z[r], att_x[r]):
            copy.start()

        @pl.when(deep - half == 1)
        def _():
            att_c[r].start()

        @pl.when(high)
        def _():
            att_h[r].start()


    kept, mate = {}, {}
    kept_z, mate_z, kept_x, mate_x = {}, {}, {}, {}
    for step, r in enumerate(order):
        kept[r] = onward(other_token(r), mine, 0, 0, step, z_to)
        mate[r] = onward(other_token(2 ^ r), near(2), 1, 1, step, z_to)
        kept_z[r] = onward(other_token(r), mine, 2, 1, step, z_to)
        mate_z[r] = onward(other_token(2 ^ r), near(2), 3, 0, step, z_to)
        kept_x[r] = onward(other_token(r), mine, 4, 2, step, x_to)
        mate_x[r] = onward(other_token(2 ^ r), near(2), 5, 3, step, x_to)

    def pass_kept():
        for r in order:
            kept[r].wait_recv()
            kept_x[r].start()

            @pl.when(half + deep < 2)
            def _():
                kept_z[r].start()

    def pass_mate():
        for r in order:
            mate[r].wait_recv()
            mate_x[r].start()

            @pl.when(half - deep == 1)
            def _():
                mate_z[r].start()

    def pass_first():
        @pl.when(half - deep == 1)
        def _():
            pass_mate()

        @pl.when(half - deep != 1)
        def _():
            pass_kept()

    def pass_second():
        @pl.when(half - deep == 1)
        def _():
            pass_kept()

        @pl.when(half - deep != 1)
        def _():
            pass_mate()

    go_exchange(0)

    @pl.when(low)
    def _():
        go_exchange(1)

    for copy in gh_near:
        copy.wait_recv()
    for step, r in enumerate(order):
        block = near(r)
        token = half * groups + block
        qc = q_buf[rows_of(block), :]
        gc = g_buf[rows_of(block), :]
        k_all = k_buf[...]
        v_all = v_buf[...]
        probs = p_buf[step]
        rounded = probs.astype(jnp.bfloat16)
        attended = att_all[rows_of(token), cols_of(mine)]
        centre = jnp.sum(
            attended.astype(jnp.float32) * gc.astype(jnp.float32), axis=1, keepdims=True
        )
        dscores = (probs * (times(gc, v_all, NT) - centre)).astype(jnp.bfloat16)
        dq = (jnp.dot(dscores, k_all, preferred_element_type=jnp.float32) * scaling).astype(
            jnp.bfloat16
        )
        if r == 0:
            dq_in[:, cols_of(mine)] = dq
        else:
            dq_send[r] = dq
            copy = remote(
                dq_send.at[r], dq_in.at[:, cols_of(mine)], dq_ssem.at[r], dq_rsem.at[r],
                (token, h),
            )
            copy.start()
            dq_near.append(copy)
        dk = times(dscores, qc, TN)
        dv = times(rounded, gc, TN)
        if step == 0:
            dk_acc[...] = dk
            dv_acc[...] = dv
        else:
            dk_acc[...] += dk
            dv_acc[...] += dv

    dk_send[...] = (dk_acc[...] * scaling).astype(jnp.bfloat16)
    dv_send[...] = dv_acc[...].astype(jnp.bfloat16)
    dk_sources = (
        (lambda to: dk_send.at[rows_of(to), :], dk_far.at[:, cols_of(mine)]),
        (lambda to: dv_send.at[rows_of(to), :], dv_far.at[:, cols_of(mine)]),
    )
    dk_cross = cross_copies(dk_sources, h, dkf_ssem, dkf_rsem)
    dk_cross_in = cross_arrivals(dk_sources, dkf_ssem, dkf_rsem)

    @pl.when(high)
    def _():
        for copy in dk_cross:
            copy.start()

    dk_near = []
    for r in range(1, groups):
        to = near(r)
        for n, (src, dst) in enumerate(((dk_send, dk_in), (dv_send, dv_in))):
            copy = remote(
                src.at[rows_of(half * groups + to), :], dst.at[:, cols_of(mine)],
                dk_ssem.at[r, n], dk_rsem.at[r, n], (half * groups + to, h),
            )
            copy.start()
            dk_near.append(copy)
    dk_in[:, cols_of(mine)] = dk_send[rows_of(s), :]
    dv_in[:, cols_of(mine)] = dv_send[rows_of(s), :]


    @pl.when(high)
    def _():
        go_exchange(1)

    fwd_near, fwd_across = {}, {}
    for step, r in enumerate(order):
        fwd_near[r] = onward(own_token(2 ^ r), near(2), 6, 4, step, x_to)
        fwd_across[r] = onward(own_token(2 ^ r), near(2), 0, 0, step, across_to)
        att_z[r].wait_recv()
        if r != 3:
            fwd_near[r].start()

        @pl.when(deep - half == 1)
        def _():
            fwd_across[r].start()


    @pl.when(half - deep == 1)
    def _():
        pass_first()

    go_moves[0][0].wait_recv()
    go_moves[0][2].start()

    @pl.when(low)
    def _():
        go_moves[1][0].wait_recv()
        go_moves[1][2].start()


    att_x[1].wait_recv()
    att_d[3].wait_recv()
    home = att_all[rows_of(s), :]

    def partial_for(head):
        return jnp.dot(home, w_buf[:, cols_of(head, lcols)], preferred_element_type=jnp.float32)

    lo_moves = [
        remote(lo_send.at[0], lo_in.at[0], lo_ssem.at[0], lo_rsem.at[0], core_to),
        remote(lo_send.at[1], lo_in.at[1], lo_ssem.at[1], lo_rsem.at[1], core_to),
        remote(lo_send.at[2], lo_in.at[2], lo_ssem.at[2], lo_rsem.at[2], y_to),
    ]
    lo_send[0] = partial_for(flip(h, 3)).astype(jnp.bfloat16)
    lo_moves[0].start()
    across = partial_for(flip(h, 2))
    lo_moves[0].wait_recv()
    lo_send[2] = (across + lo_in[0].astype(jnp.float32)).astype(jnp.bfloat16)
    lo_moves[2].start()
    lo_send[1] = partial_for(flip(h, 1)).astype(jnp.bfloat16)
    lo_moves[1].start()
    layer = partial_for(h)


    @pl.when(half - deep == 1)
    def _():
        pass_second()


    @pl.when(half + deep == 2)
    def _():
        pass_first()


    @pl.when(half + deep == 2)
    def _():
        pass_second()


    @pl.when(low)
    def _():
        pass_first()


    @pl.when(low)
    def _():
        pass_second()

    def weight_rows(bits):
        head = near(bits)
        gw_out[rows_of(head), :] = times(
            att_all[:, cols_of(head)], go_all[...].reshape(seqs * rows, gcols), TN
        )


    @pl.when(high)
    def _():
        go_moves[1][0].wait_recv()
        go_moves[1][2].start()

    for n in range(2):
        go_moves[n][1].wait_recv()
        go_moves[n][2].wait_recv()
    weight_rows(0)
    weight_rows(2)
    for copy in dq_near:
        copy.wait_recv()
    gq_out[...] = dq_in[...]
    lo_moves[1].wait_recv()
    lo_moves[2].wait_recv()
    lo_out[...] = (layer + lo_in[1].astype(jnp.float32) + lo_in[2].astype(jnp.float32)).astype(
        jnp.bfloat16
    )
    for r in order:
        if r != 1:
            att_x[r].wait_recv()
        kept_x[r].wait_recv()
    weight_rows(1)
    for copy in dk_near:
        copy.wait_recv()

    @pl.when(low)
    def _():
        for copy in dk_cross_in:
            copy.wait_recv()

    gk_out[...] = (dk_in[...].astype(jnp.float32) + dk_far[...].astype(jnp.float32)).astype(
        jnp.bfloat16
    )
    gv_out[...] = (dv_in[...].astype(jnp.float32) + dv_far[...].astype(jnp.float32)).astype(
        jnp.bfloat16
    )
    for r in order:
        if r != 3:
            fwd_near[r].wait_recv()
        mate_x[r].wait_recv()
    weight_rows(3)

    moved = inside + gh_near + spread + go_moves[0] + go_moves[1] + dq_near + dk_near + lo_moves
    del fwd_near[3]
    for group in (att_x, att_z, att_d, fwd_near, kept_x, mate_x):
        moved += list(group.values())
    for copy in moved:
        copy.wait_send()

    @pl.when(deep - half == 1)
    def _():
        for group in (att_c, fwd_across):
            for copy in group.values():
                copy.wait_send()

    @pl.when(high)
    def _():
        for copy in att_h.values():
            copy.wait_send()

    @pl.when(half + deep < 2)
    def _():
        for copy in kept_z.values():
            copy.wait_send()

    @pl.when(half - deep == 1)
    def _():
        for copy in mate_z.values():
            copy.wait_send()

    @pl.when(low)
    def _():
        for copy in far:
            copy.wait_send()

    @pl.when(high)
    def _():
        for copy in dk_cross:
            copy.wait_send()


def place_kernel(*refs):
    sem = refs[-1]
    half = len(refs) // 2
    copies = [
        pltpu.make_async_copy(refs[n], refs[half + n], sem.at[n]) for n in range(half)
    ]
    for copy in copies:
        copy.start()
    for copy in copies:
        copy.wait()


def dense_device(queries, keys, values, bucket, w_out, grad_out):
    seqs = lax.axis_size("seq")
    heads = lax.axis_size("head")
    rows, features = queries.shape
    model = w_out.shape[1]
    groups = features // HSZ
    part = groups * rows
    tokens = seqs * rows
    bf, f32 = jnp.bfloat16, jnp.float32
    vmem = pl.BlockSpec(memory_space=pltpu.VMEM)
    hbm = pl.BlockSpec(memory_space=pl.ANY)
    dma = pltpu.SemaphoreType.DMA
    wide = pltpu.VMEM((rows, features), bf)
    sems = []
    for shape in (
        (groups, 4), (groups, 2), (seqs,), (6,), (4, groups), (7, groups), (groups,), (groups, 2),
        (groups, 2), (3,),
    ):
        sems += [dma(shape), dma(shape)]
    shapes = (
        ((rows, model // heads), bf),
        ((rows, features), bf),
        ((rows, features), bf),
        ((rows, features), bf),
        ((features, model // seqs), f32),
    )
    made = pl.pallas_call(
        functools.partial(dense_kernel, seqs, heads),
        out_shape=tuple(pltpu.VMEM(shape, dtype) for shape, dtype in shapes),
        in_specs=[hbm, hbm, hbm, vmem, hbm, hbm],
        out_specs=(vmem,) * 5,
        scratch_shapes=[
            pltpu.VMEM(w_out.shape, bf),
            pltpu.VMEM(grad_out.shape, bf),
            wide,
            pltpu.VMEM((part, HSZ), bf),
            pltpu.VMEM((part, HSZ), bf),
            pltpu.VMEM((tokens, HSZ), bf),
            pltpu.VMEM((tokens, HSZ), bf),
            pltpu.VMEM((seqs, rows, model // seqs), bf),
            pltpu.VMEM((tokens, features), bf),
            pltpu.VMEM((groups, rows, HSZ), bf),
            pltpu.VMEM((tokens, HSZ), f32),
            pltpu.VMEM((tokens, HSZ), f32),
            pltpu.VMEM((tokens, HSZ), bf),
            pltpu.VMEM((tokens, HSZ), bf),
            wide,
            wide,
            wide,
            wide,
            wide,
            pltpu.VMEM((3, rows, model // heads), bf),
            pltpu.VMEM((3, rows, model // heads), bf),
            pltpu.VMEM((groups, rows, tokens), f32),
            dma((6,)),
        ]
        + sems,
        compiler_params=pltpu.CompilerParams(
            collective_id=0, has_side_effects=True, vmem_limit_bytes=58 * 2**20
        ),
    )(queries, keys, values, bucket.reshape(1, -1), w_out, grad_out)
    return pl.pallas_call(
        place_kernel,
        out_shape=tuple(jax.ShapeDtypeStruct(shape, dtype) for shape, dtype in shapes),
        in_specs=[vmem] * 5,
        out_specs=(hbm,) * 5,
        scratch_shapes=[dma((5,))],
    )(*[pltpu.with_memory_space_constraint(one, pltpu.VMEM) for one in made])


def choose(queries, keys, values, bucket, w_out, grad_out):
    groups = queries.shape[1] // HSZ
    dense = groups == 4 and lax.axis_size("seq") == 8 and lax.axis_size("head") == 4
    plan = dense_device if dense else per_device
    return plan(queries, keys, values, bucket, w_out, grad_out)


def solution(mesh):
    return jax.shard_map(
        choose,
        mesh=mesh,
        in_specs=(
            P("seq", "head"),
            P("seq", "head"),
            P("seq", "head"),
            P(),
            P("head", None),
            P("seq", None),
        ),
        out_specs=(
            P("seq", "head"),
            P("seq", "head"),
            P("seq", "head"),
            P("seq", "head"),
            P("head", "seq"),
        ),
        check_vma=False,
    )
```

```python
import functools
import math

import jax
import jax.numpy as jnp
from jax import lax
from jax.experimental import pallas as pl
from jax.experimental.pallas import tpu as pltpu
from jax.sharding import PartitionSpec as P

HSZ = 128


def passed_along(value, axis, by):
    length = lax.axis_size(axis)
    pairs = [(i, i + by) for i in range(length) if 0 <= i + by < length]
    return lax.ppermute(value, axis, pairs)


def earlier_count(flags, axis):
    length = flags.shape[axis]
    at = jnp.arange(length)
    if axis == 0:
        before = (at[None, :] < at[:, None]).astype(jnp.float32)
        return jnp.dot(before, flags.astype(jnp.float32)).astype(jnp.int32)
    before = (at[:, None] < at[None, :]).astype(jnp.float32)
    return jnp.dot(flags.astype(jnp.float32), before).astype(jnp.int32)


def member_table(bucket_grid, owner, slot_count):
    matches = (bucket_grid == owner).astype(jnp.int32)
    ranking = earlier_count(matches, 1)
    slot_ids = jnp.arange(slot_count, dtype=jnp.int32)
    placed = matches[:, :, None] * (ranking[:, :, None] == slot_ids[None, None, :]).astype(
        jnp.int32
    )
    sources = bucket_grid.shape[0]
    stride = bucket_grid.shape[1]
    offsets = (
        jnp.arange(sources, dtype=jnp.int32)[:, None] * stride
        + jnp.arange(stride, dtype=jnp.int32)[None, :]
    )
    where_at = jnp.sum(placed * offsets[:, :, None], axis=1).reshape(-1)
    present = jnp.sum(placed, axis=1).reshape(-1)
    return (where_at, present)


def allowed_mask(where_here, alive_here, where_before, alive_before):
    amount = where_here.shape[0]
    asking = alive_here[:, None] > 0
    inside = (where_here[None, :] <= where_here[:, None]) & (alive_here[None, :] > 0) & asking
    inside = inside | (jnp.arange(amount)[:, None] == jnp.arange(amount)[None, :])
    earlier = (where_before[None, :] <= where_here[:, None]) & (alive_before[None, :] > 0) & asking
    return jnp.concatenate([inside, earlier], axis=1)


def softmax_rows(scores, allowed):
    masked = jnp.where(allowed[None], scores, -1e30)
    largest = jnp.max(masked, axis=2, keepdims=True)
    weights = jnp.where(allowed[None], jnp.exp(masked - largest), 0.0)
    return weights / jnp.sum(weights, axis=2, keepdims=True)


def local_slots(bucket_grid, device, sources, slot_total):
    my_buckets = lax.dynamic_index_in_dim(bucket_grid, device, 0, keepdims=False)
    owners = jnp.arange(sources, dtype=jnp.int32)
    onehot = (my_buckets[:, None] == owners[None, :]).astype(jnp.int32)
    ranking = jnp.sum(earlier_count(onehot, 0) * onehot, axis=1)
    back_index = my_buckets * slot_total + ranking
    slot_ids = jnp.arange(slot_total, dtype=jnp.int32)
    placed = onehot[:, :, None] * (ranking[:, None, None] == slot_ids[None, None, :]).astype(
        jnp.int32
    )
    token_ids = jnp.arange(my_buckets.shape[0], dtype=jnp.int32)
    send_index = jnp.sum(placed * token_ids[:, None, None], axis=0).reshape(-1)
    send_live = jnp.sum(placed, axis=0).reshape(-1)
    return (back_index, send_index, send_live)


def owner_probs(query_rows, key_all, allowed, scaling):
    scores = (
        jnp.einsum("qgd,kgd->gqk", query_rows, key_all, preferred_element_type=jnp.float32)
        * scaling
    )
    return softmax_rows(scores, allowed)


def owner_forward(probs, value_all):
    rounded = probs.astype(jnp.bfloat16)
    attended = jnp.einsum(
        "gqk,kgd->qgd", rounded, value_all, preferred_element_type=jnp.float32
    ).astype(jnp.bfloat16)
    return (rounded, attended)


def owner_backward(probs, rounded, attended, grad_rows, query_rows, key_all, value_all, scaling):
    centre = jnp.sum(attended.astype(jnp.float32) * grad_rows.astype(jnp.float32), axis=2)
    dprobs = jnp.einsum("qgd,kgd->gqk", grad_rows, value_all, preferred_element_type=jnp.float32)
    dscores = probs * (dprobs - jnp.transpose(centre)[:, :, None])
    dround = dscores.astype(jnp.bfloat16)
    grad_query = (
        jnp.einsum("gqk,kgd->qgd", dround, key_all, preferred_element_type=jnp.float32) * scaling
    ).astype(jnp.bfloat16)
    grad_key = (
        jnp.einsum("gqk,qgd->kgd", dround, query_rows, preferred_element_type=jnp.float32) * scaling
    )
    grad_value = jnp.einsum("gqk,qgd->kgd", rounded, grad_rows, preferred_element_type=jnp.float32)
    return (grad_query, grad_key, grad_value)


def with_previous(key_rows, value_rows):
    key_before, value_before = passed_along((key_rows, value_rows), "seq", 1)
    return (
        jnp.concatenate([key_rows, key_before], axis=0),
        jnp.concatenate([value_rows, value_before], axis=0),
    )


def settle_keys(grad_key, grad_value, slot_rows):
    key_next, value_next = passed_along(
        (grad_key[slot_rows:].astype(jnp.bfloat16), grad_value[slot_rows:].astype(jnp.bfloat16)),
        "seq",
        -1,
    )
    key_total = (grad_key[:slot_rows] + key_next.astype(jnp.float32)).astype(jnp.bfloat16)
    value_total = (grad_value[:slot_rows] + value_next.astype(jnp.float32)).astype(jnp.bfloat16)
    return (key_total, value_total)


def per_device(queries, keys, values, bucket, w_out, grad_out):
    sources = lax.axis_size("seq")
    device = lax.axis_index("seq")
    token_rows = queries.shape[0]
    features = queries.shape[1]
    groups = features // HSZ
    slot_total = max(2, 3 * token_rows // (2 * sources))
    slot_rows = sources * slot_total
    scaling = 1.0 / math.sqrt(HSZ)
    bucket_grid = bucket[:, 0].reshape(sources, token_rows)
    back_index, send_index, send_live = local_slots(bucket_grid, device, sources, slot_total)
    where_here, alive_here = member_table(bucket_grid, device, slot_total)
    where_before, alive_before = member_table(bucket_grid, device - 1, slot_total)
    allowed = allowed_mask(where_here, alive_here, where_before, alive_before)
    grad_heads = lax.dot_general(
        grad_out, w_out, (((1,), (1,)), ((), ())), preferred_element_type=jnp.float32
    ).astype(jnp.bfloat16)

    def pack_rows(source):
        return jnp.take(source, send_index, axis=0) * send_live[:, None].astype(source.dtype)

    def split_heads(block):
        return block.reshape(block.shape[0], groups, HSZ)

    def flatten(block):
        return block.reshape(block.shape[0], features)

    query_rows, key_rows, value_rows = (
        lax.all_to_all(pack_rows(queries), "seq", split_axis=0, concat_axis=0, tiled=True),
        lax.all_to_all(pack_rows(keys), "seq", split_axis=0, concat_axis=0, tiled=True),
        lax.all_to_all(pack_rows(values), "seq", split_axis=0, concat_axis=0, tiled=True),
    )
    key_all, value_all = with_previous(key_rows, value_rows)
    probs = owner_probs(split_heads(query_rows), split_heads(key_all), allowed, scaling)
    rounded, attended = owner_forward(probs, split_heads(value_all))
    key_all, value_all, probs, rounded, attended = (key_all, value_all, probs, rounded, attended)
    returned = lax.all_to_all(flatten(attended), "seq", split_axis=0, concat_axis=0, tiled=True)
    grad_rows = lax.all_to_all(
        pack_rows(grad_heads), "seq", split_axis=0, concat_axis=0, tiled=True
    )
    grad_query, grad_key, grad_value = owner_backward(
        probs,
        rounded,
        attended,
        split_heads(grad_rows),
        split_heads(query_rows),
        split_heads(key_all),
        split_heads(value_all),
        scaling,
    )
    key_total, value_total = settle_keys(flatten(grad_key), flatten(grad_value), slot_rows)
    back_query, back_key, back_value = (
        lax.all_to_all(flatten(grad_query), "seq", split_axis=0, concat_axis=0, tiled=True),
        lax.all_to_all(key_total, "seq", split_axis=0, concat_axis=0, tiled=True),
        lax.all_to_all(value_total, "seq", split_axis=0, concat_axis=0, tiled=True),
    )
    attended_home = jnp.take(returned, back_index, axis=0)
    partial_value = jnp.dot(attended_home, w_out, preferred_element_type=jnp.float32)
    layer_out = lax.psum_scatter(
        partial_value.astype(jnp.bfloat16), "head", scatter_dimension=1, tiled=True
    )
    weight_terms = lax.dot_general(
        attended_home, grad_out, (((0,), (0,)), ((), ())), preferred_element_type=jnp.float32
    )
    grad_weight = lax.psum_scatter(weight_terms, "seq", scatter_dimension=1, tiled=True)
    grad_queries = jnp.take(back_query, back_index, axis=0)
    grad_keys = jnp.take(back_key, back_index, axis=0)
    grad_values = jnp.take(back_value, back_index, axis=0)
    return (layer_out, grad_queries, grad_keys, grad_values, grad_weight)


MESH = pl.DeviceIdType.MESH
NT = (((1,), (1,)), ((), ()))
TN = (((0,), (0,)), ((), ()))


def times(a, b, dims):
    return lax.dot_general(a, b, dims, preferred_element_type=jnp.float32)


def dense_kernel(
    seqs,
    heads,
    q_hbm,
    k_hbm,
    v_hbm,
    brow,
    w_hbm,
    go_hbm,
    lo_out,
    gq_out,
    gk_out,
    gv_out,
    gw_out,
    w_buf,
    go_buf,
    gh_buf,
    q_buf,
    g_buf,
    k_buf,
    v_buf,
    go_all,
    att_all,
    dq_send,
    dk_acc,
    dv_acc,
    dk_send,
    dv_send,
    dq_in,
    dk_in,
    dv_in,
    dk_far,
    dv_far,
    lo_send,
    lo_in,
    p_buf,
    local_sem,
    in_send,
    in_recv,
    far_send,
    far_recv,
    go_send,
    go_recv,
    gx_send,
    gx_recv,
    att_send,
    att_recv,
    fwd_send,
    fwd_recv,
    dq_ssem,
    dq_rsem,
    dk_ssem,
    dk_rsem,
    dkf_ssem,
    dkf_rsem,
    lo_ssem,
    lo_rsem,
):
    s = lax.axis_index("seq")
    h = lax.axis_index("head")
    rows = q_hbm.shape[0]
    width = HSZ
    groups = q_hbm.shape[1] // width
    half = lax.div(s, groups)
    mine = lax.rem(s, groups)
    part = groups * rows
    scaling = 1.0 / math.sqrt(HSZ)
    gcols = w_hbm.shape[1] // seqs
    lcols = w_hbm.shape[1] // heads
    quarter = rows // heads
    low = half == 0
    high = half == 1
    deep = lax.div(mine, 2)

    def flip(index, bits):
        out = index
        for bit in (1, 2, 4):
            if bits & bit:
                out = out + bit * (1 - 2 * lax.rem(lax.div(index, bit), 2))
        return out

    def near(r):
        return flip(mine, r)

    def rows_of(block):
        return pl.ds(pl.multiple_of(block * rows, rows), rows)

    def cols_of(block, size=width):
        return pl.ds(pl.multiple_of(block * size, size), size)

    def quarter_of(head):
        return pl.ds(pl.multiple_of(head * quarter, quarter), quarter)

    def remote(src, dst, ssem, rsem, where):
        return pltpu.make_async_remote_copy(
            src_ref=src, dst_ref=dst, send_sem=ssem, recv_sem=rsem, device_id=where,
            device_id_type=MESH,
        )

    x_to, z_to, d_to = (flip(s, 1), h), (flip(s, 2), h), (flip(s, 3), h)
    c_to, across_to = (flip(s, 4), h), (s + 2 - 4 * half, h)
    core_to, y_to = (s, flip(h, 1)), (s, flip(h, 2))

    w_copy = pltpu.make_async_copy(w_hbm, w_buf, local_sem.at[0])
    go_copy = pltpu.make_async_copy(go_hbm, go_buf, local_sem.at[1])
    go_copy.start()
    w_copy.start()
    own = [
        pltpu.make_async_copy(k_hbm.at[:, cols_of(mine)], k_buf.at[rows_of(s), :], local_sem.at[2]),
        pltpu.make_async_copy(v_hbm.at[:, cols_of(mine)], v_buf.at[rows_of(s), :], local_sem.at[3]),
        pltpu.make_async_copy(q_hbm.at[:, cols_of(mine)], q_buf.at[rows_of(mine), :], local_sem.at[4]),
    ]
    for copy in own:
        copy.start()
    go_own = pltpu.make_async_copy(
        go_hbm.at[quarter_of(h), cols_of(s, gcols)], go_all.at[s, quarter_of(h), :], local_sem.at[5]
    )
    go_own.start()

    barrier = pltpu.get_barrier_semaphore()
    for r in range(1, seqs):
        pl.semaphore_signal(
            barrier, inc=1, device_id=(lax.rem(s + r, seqs), h), device_id_type=MESH
        )
    for there in (core_to, y_to):
        pl.semaphore_signal(barrier, inc=1, device_id=there, device_id_type=MESH)
    pl.semaphore_wait(barrier, seqs + 1)

    def cross_copies(sources, there_in, ssem, rsem):
        out = []
        for block in range(2):
            for side in range(2):
                to = 2 * block + lax.rem(mine + side, 2)
                for n, (src, dst) in enumerate(sources):
                    out.append(
                        remote(
                            src(to), dst, ssem.at[2 * block + side, n],
                            rsem.at[2 * deep + side, n], ((1 - half) * groups + to, there_in),
                        )
                    )
        return out

    def cross_arrivals(sources, ssem, rsem):
        return [
            remote(src(mine), dst, ssem.at[r, n], rsem.at[r, n], c_to)
            for r in range(groups)
            for n, (src, dst) in enumerate(sources)
        ]

    far_sources = (
        (lambda to: k_hbm.at[:, cols_of(to)], k_buf.at[rows_of(s), :]),
        (lambda to: v_hbm.at[:, cols_of(to)], v_buf.at[rows_of(s), :]),
    )
    far = cross_copies(far_sources, h, far_send, far_recv)
    far_in = cross_arrivals(far_sources, far_send, far_recv)

    @pl.when(low)
    def _():
        for copy in far[:4]:
            copy.start()

    inside = []
    for n, (src, dst, at) in enumerate(
        ((k_hbm, k_buf, s), (q_hbm, q_buf, mine), (v_hbm, v_buf, s))
    ):
        for r in (3, 2, 1):
            to = near(r)
            copy = remote(
                src.at[:, cols_of(to)], dst.at[rows_of(at), :], in_send.at[r, n],
                in_recv.at[r, n], (half * groups + to, h),
            )
            copy.start()
            inside.append(copy)
    spread = []
    for r in range(1, seqs):
        to = lax.rem(s + r, seqs)
        spread.append(
            remote(
                go_hbm.at[quarter_of(h), cols_of(to, gcols)], go_all.at[s, quarter_of(h), :],
                go_send.at[r], go_recv.at[s], (to, h),
            )
        )
    spread_in = [
        remote(
            go_hbm.at[quarter_of(h), cols_of(s, gcols)], go_all.at[source, quarter_of(h), :],
            go_send.at[0], go_recv.at[source], x_to,
        )
        for source in range(seqs)
    ]

    @pl.when(low)
    def _():
        for copy in far[4:]:
            copy.start()

    @pl.when(high)
    def _():
        for copy in spread:
            copy.start()

    @pl.when(high)
    def _():
        dk_far[...] = jnp.zeros_like(dk_far)
        dv_far[...] = jnp.zeros_like(dv_far)

    go_copy.wait()
    w_copy.wait()
    depth = w_buf.shape[1] // seqs

    def heads_step(c, total):
        at = pl.ds(pl.multiple_of(c * depth, depth), depth)
        return total + times(go_buf[:, at], w_buf[:, at], NT)

    gh = lax.fori_loop(
        0, seqs, heads_step, jnp.zeros((rows, groups * width), jnp.float32)
    )
    gh_buf[...] = gh.astype(jnp.bfloat16)
    gh_near = []
    for r in (3, 2, 1):
        to = near(r)
        copy = remote(
            gh_buf.at[:, cols_of(to)], g_buf.at[rows_of(mine), :], in_send.at[r, 3],
            in_recv.at[r, 3], (half * groups + to, h),
        )
        copy.start()
        gh_near.append(copy)
    g_buf[rows_of(mine), :] = gh_buf[:, cols_of(mine)]

    @pl.when(low)
    def _():
        for copy in spread:
            copy.start()

    for copy in own:
        copy.wait()
    for copy in inside:
        copy.wait_recv()

    @pl.when(high)
    def _():
        for copy in far_in:
            copy.wait_recv()

    def piece(token, head, kind, there):
        at = att_all.at[rows_of(token), cols_of(head)]
        lane, step = kind
        return remote(at, at, att_send.at[lane, step], att_recv.at[lane, step], there)

    def onward(token, head, out, into, step, there):
        at = att_all.at[rows_of(token), cols_of(head)]
        return remote(at, at, fwd_send.at[out, step], fwd_recv.at[into, step], there)

    def own_token(bits):
        return half * groups + near(bits)

    def other_token(bits):
        return (1 - half) * groups + near(bits)

    diagonal = lax.broadcasted_iota(jnp.int32, (rows, rows), 0) == lax.broadcasted_iota(
        jnp.int32, (rows, rows), 1
    )
    order = (3, 1, 2, 0)
    def go_part(first, head, index, where):
        at = go_all.at[pl.ds(first, groups), quarter_of(head), :]
        return remote(at, at, gx_send.at[index], gx_recv.at[index], where)

    go_moves = [
        [
            go_part(first, h, 3 * n, y_to),
            go_part(first, h, 3 * n + 1, core_to),
            go_part(first, flip(h, 2), 3 * n + 2, core_to),
        ]
        for n, first in enumerate((groups, 0))
    ]

    def go_exchange(n):
        first = (groups, 0)[n]

        @pl.when(half == 1 - n)
        def _():
            go_own.wait()

        for source in range(first, first + groups):

            @pl.when(s != source)
            def _():
                spread_in[source].wait_recv()

        go_moves[n][0].start()
        go_moves[n][1].start()

    att_x, att_z, att_c, att_h, att_d = {}, {}, {}, {}, {}
    dq_near = []
    def forward(step, block, token, span):
        qc = q_buf[rows_of(block), :]
        k_all = k_buf[:span, :]
        v_all = v_buf[:span, :]
        along = brow[:, cols_of(token, rows)].astype(jnp.float32)
        gap = jnp.sum(jnp.where(diagonal, along, 0.0), axis=1, keepdims=True)
        gap = gap - brow[:, :span].astype(jnp.float32)
        keys_at = lax.broadcasted_iota(jnp.int32, (rows, span), 1)
        query_at = token * rows + lax.broadcasted_iota(jnp.int32, (rows, span), 0)
        allowed = ((gap == 0.0) | (gap == 1.0)) & (keys_at <= query_at)
        scores = jnp.where(allowed, times(qc, k_all, NT) * scaling, -1e30)
        largest = jnp.max(scores, axis=1, keepdims=True)
        weights = jnp.where(allowed, jnp.exp(scores - largest), 0.0)
        probs = weights * (1.0 / jnp.sum(weights, axis=1, keepdims=True))
        p_buf[step, :, :span] = probs
        att_all[rows_of(token), cols_of(mine)] = jnp.dot(
            probs.astype(jnp.bfloat16), v_all, preferred_element_type=jnp.float32
        ).astype(jnp.bfloat16)

    def backward(step, block, token, span, dq_to):
        qc = q_buf[rows_of(block), :]
        gc = g_buf[rows_of(block), :]
        k_all = k_buf[:span, :]
        probs = p_buf[step, :, :span]
        attended = att_all[rows_of(token), cols_of(mine)]
        centre = jnp.sum(
            attended.astype(jnp.float32) * gc.astype(jnp.float32), axis=1, keepdims=True
        )
        dscores = (probs * (times(gc, v_buf[:span, :], NT) - centre)).astype(jnp.bfloat16)
        dq_to[...] = (
            jnp.dot(dscores, k_all, preferred_element_type=jnp.float32) * scaling
        ).astype(jnp.bfloat16)
        dk = times(dscores, qc, TN)
        dv = times(probs.astype(jnp.bfloat16), gc, TN)
        if step == 0:
            dk_acc[:span, :] = dk
            dv_acc[:span, :] = dv
        else:
            dk_acc[:span, :] += dk
            dv_acc[:span, :] += dv

    def by_half(work, *args):
        @pl.when(low)
        def _():
            work(part, *args)

        @pl.when(high)
        def _():
            work(2 * part, *args)

    for step, r in enumerate(order):
        block = near(r)
        token = half * groups + block
        by_half(lambda span, step=step, block=block, token=token: forward(step, block, token, span))
        if r == 3:
            att_d[r] = piece(token, mine, (3, step), d_to)
            att_d[r].start()
        att_c[r] = onward(token, mine, 1, 1, step, across_to)
        att_h[r] = onward(token, mine, 1, 0, step, c_to)
        att_z[r] = piece(token, mine, (1, step), z_to)
        att_x[r] = piece(token, mine, (0, step), x_to)
        for copy in (att_z[r], att_x[r]):
            copy.start()

        @pl.when(deep - half == 1)
        def _():
            att_c[r].start()

        @pl.when(high)
        def _():
            att_h[r].start()


    kept, mate = {}, {}
    kept_z, mate_z, kept_x, mate_x = {}, {}, {}, {}
    for step, r in enumerate(order):
        kept[r] = onward(other_token(r), mine, 0, 0, step, z_to)
        mate[r] = onward(other_token(2 ^ r), near(2), 1, 1, step, z_to)
        kept_z[r] = onward(other_token(r), mine, 2, 1, step, z_to)
        mate_z[r] = onward(other_token(2 ^ r), near(2), 3, 0, step, z_to)
        kept_x[r] = onward(other_token(r), mine, 4, 2, step, x_to)
        mate_x[r] = onward(other_token(2 ^ r), near(2), 5, 3, step, x_to)

    def pass_kept():
        for r in order:
            kept[r].wait_recv()
            kept_x[r].start()

            @pl.when(half + deep < 2)
            def _():
                kept_z[r].start()

    def pass_mate():
        for r in order:
            mate[r].wait_recv()
            mate_x[r].start()

            @pl.when(half - deep == 1)
            def _():
                mate_z[r].start()

    def pass_first():
        @pl.when(half - deep == 1)
        def _():
            pass_mate()

        @pl.when(half - deep != 1)
        def _():
            pass_kept()

    def pass_second():
        @pl.when(half - deep == 1)
        def _():
            pass_kept()

        @pl.when(half - deep != 1)
        def _():
            pass_mate()

    go_exchange(0)

    @pl.when(low)
    def _():
        go_exchange(1)

    for copy in gh_near:
        copy.wait_recv()
    for step, r in enumerate(order):
        block = near(r)
        token = half * groups + block
        dq_to = dq_in.at[:, cols_of(mine)] if r == 0 else dq_send.at[r]
        by_half(
            lambda span, step=step, block=block, token=token, dq_to=dq_to: backward(
                step, block, token, span, dq_to
            )
        )
        if r != 0:
            copy = remote(
                dq_send.at[r], dq_in.at[:, cols_of(mine)], dq_ssem.at[r], dq_rsem.at[r],
                (token, h),
            )
            copy.start()
            dq_near.append(copy)

    def round_terms(span):
        dk_send[:span, :] = (dk_acc[:span, :] * scaling).astype(jnp.bfloat16)
        dv_send[:span, :] = dv_acc[:span, :].astype(jnp.bfloat16)

    by_half(round_terms)
    dk_sources = (
        (lambda to: dk_send.at[rows_of(to), :], dk_far.at[:, cols_of(mine)]),
        (lambda to: dv_send.at[rows_of(to), :], dv_far.at[:, cols_of(mine)]),
    )
    dk_cross = cross_copies(dk_sources, h, dkf_ssem, dkf_rsem)
    dk_cross_in = cross_arrivals(dk_sources, dkf_ssem, dkf_rsem)


    dk_near = []
    for r in range(1, groups):
        to = near(r)
        for n, (src, dst) in enumerate(((dk_send, dk_in), (dv_send, dv_in))):
            copy = remote(
                src.at[rows_of(half * groups + to), :], dst.at[:, cols_of(mine)],
                dk_ssem.at[r, n], dk_rsem.at[r, n], (half * groups + to, h),
            )
            copy.start()
            dk_near.append(copy)
    @pl.when(high)
    def _():
        for copy in dk_cross:
            copy.start()

    dk_in[:, cols_of(mine)] = dk_send[rows_of(s), :]
    dv_in[:, cols_of(mine)] = dv_send[rows_of(s), :]


    @pl.when(high)
    def _():
        go_exchange(1)

    fwd_near, fwd_across = {}, {}
    for step, r in enumerate(order):
        fwd_near[r] = onward(own_token(2 ^ r), near(2), 6, 4, step, x_to)
        fwd_across[r] = onward(own_token(2 ^ r), near(2), 0, 0, step, across_to)
        att_z[r].wait_recv()
        if r != 3:
            fwd_near[r].start()

        @pl.when(deep - half == 1)
        def _():
            fwd_across[r].start()


    @pl.when(half - deep == 1)
    def _():
        pass_first()

    go_moves[0][0].wait_recv()
    go_moves[0][2].start()

    @pl.when(low)
    def _():
        go_moves[1][0].wait_recv()
        go_moves[1][2].start()


    att_x[1].wait_recv()
    att_d[3].wait_recv()
    home = att_all[rows_of(s), :]

    def partial_for(head):
        return jnp.dot(home, w_buf[:, cols_of(head, lcols)], preferred_element_type=jnp.float32)

    lo_moves = [
        remote(lo_send.at[0], lo_in.at[0], lo_ssem.at[0], lo_rsem.at[0], core_to),
        remote(lo_send.at[1], lo_in.at[1], lo_ssem.at[1], lo_rsem.at[1], core_to),
        remote(lo_send.at[2], lo_in.at[2], lo_ssem.at[2], lo_rsem.at[2], y_to),
    ]
    lo_send[0] = partial_for(flip(h, 3)).astype(jnp.bfloat16)
    lo_moves[0].start()
    across = partial_for(flip(h, 2))
    lo_moves[0].wait_recv()
    lo_send[2] = (across + lo_in[0].astype(jnp.float32)).astype(jnp.bfloat16)
    lo_moves[2].start()
    lo_send[1] = partial_for(flip(h, 1)).astype(jnp.bfloat16)
    lo_moves[1].start()
    layer = partial_for(h)


    @pl.when(half - deep == 1)
    def _():
        pass_second()


    @pl.when(half + deep == 2)
    def _():
        pass_first()


    @pl.when(half + deep == 2)
    def _():
        pass_second()


    @pl.when(low)
    def _():
        pass_first()


    @pl.when(low)
    def _():
        pass_second()

    def weight_rows(bits):
        head = near(bits)
        gw_out[rows_of(head), :] = times(
            att_all[:, cols_of(head)], go_all[...].reshape(seqs * rows, gcols), TN
        )


    @pl.when(high)
    def _():
        go_moves[1][0].wait_recv()
        go_moves[1][2].start()

    for n in range(2):
        go_moves[n][1].wait_recv()
        go_moves[n][2].wait_recv()
    weight_rows(0)
    weight_rows(2)
    for copy in dq_near:
        copy.wait_recv()
    gq_out[...] = dq_in[...]
    lo_moves[1].wait_recv()
    lo_moves[2].wait_recv()
    lo_out[...] = (layer + lo_in[1].astype(jnp.float32) + lo_in[2].astype(jnp.float32)).astype(
        jnp.bfloat16
    )
    for r in order:
        if r != 1:
            att_x[r].wait_recv()
        kept_x[r].wait_recv()
    weight_rows(1)
    for r in order:
        if r != 3:
            fwd_near[r].wait_recv()
        mate_x[r].wait_recv()
    weight_rows(3)
    for copy in dk_near:
        copy.wait_recv()

    @pl.when(low)
    def _():
        for copy in dk_cross_in:
            copy.wait_recv()

    gk_out[...] = (dk_in[...].astype(jnp.float32) + dk_far[...].astype(jnp.float32)).astype(
        jnp.bfloat16
    )
    gv_out[...] = (dv_in[...].astype(jnp.float32) + dv_far[...].astype(jnp.float32)).astype(
        jnp.bfloat16
    )

    moved = inside + gh_near + spread + go_moves[0] + go_moves[1] + dq_near + dk_near + lo_moves
    del fwd_near[3]
    for group in (att_x, att_z, att_d, fwd_near, kept_x, mate_x):
        moved += list(group.values())
    for copy in moved:
        copy.wait_send()

    @pl.when(deep - half == 1)
    def _():
        for group in (att_c, fwd_across):
            for copy in group.values():
                copy.wait_send()

    @pl.when(high)
    def _():
        for copy in att_h.values():
            copy.wait_send()

    @pl.when(half + deep < 2)
    def _():
        for copy in kept_z.values():
            copy.wait_send()

    @pl.when(half - deep == 1)
    def _():
        for copy in mate_z.values():
            copy.wait_send()

    @pl.when(low)
    def _():
        for copy in far:
            copy.wait_send()

    @pl.when(high)
    def _():
        for copy in dk_cross:
            copy.wait_send()


def place_kernel(*refs):
    sem = refs[-1]
    half = len(refs) // 2
    copies = [
        pltpu.make_async_copy(refs[n], refs[half + n], sem.at[n]) for n in range(half)
    ]
    for copy in copies:
        copy.start()
    for copy in copies:
        copy.wait()


def dense_device(queries, keys, values, bucket, w_out, grad_out):
    seqs = lax.axis_size("seq")
    heads = lax.axis_size("head")
    rows, features = queries.shape
    model = w_out.shape[1]
    groups = features // HSZ
    part = groups * rows
    tokens = seqs * rows
    bf, f32 = jnp.bfloat16, jnp.float32
    vmem = pl.BlockSpec(memory_space=pltpu.VMEM)
    hbm = pl.BlockSpec(memory_space=pl.ANY)
    dma = pltpu.SemaphoreType.DMA
    wide = pltpu.VMEM((rows, features), bf)
    sems = []
    for shape in (
        (groups, 4), (groups, 2), (seqs,), (6,), (4, groups), (7, groups), (groups,), (groups, 2),
        (groups, 2), (3,),
    ):
        sems += [dma(shape), dma(shape)]
    shapes = (
        ((rows, model // heads), bf),
        ((rows, features), bf),
        ((rows, features), bf),
        ((rows, features), bf),
        ((features, model // seqs), f32),
    )
    made = pl.pallas_call(
        functools.partial(dense_kernel, seqs, heads),
        out_shape=tuple(pltpu.VMEM(shape, dtype) for shape, dtype in shapes),
        in_specs=[hbm, hbm, hbm, vmem, hbm, hbm],
        out_specs=(vmem,) * 5,
        scratch_shapes=[
            pltpu.VMEM(w_out.shape, bf),
            pltpu.VMEM(grad_out.shape, bf),
            wide,
            pltpu.VMEM((part, HSZ), bf),
            pltpu.VMEM((part, HSZ), bf),
            pltpu.VMEM((tokens, HSZ), bf),
            pltpu.VMEM((tokens, HSZ), bf),
            pltpu.VMEM((seqs, rows, model // seqs), bf),
            pltpu.VMEM((tokens, features), bf),
            pltpu.VMEM((groups, rows, HSZ), bf),
            pltpu.VMEM((tokens, HSZ), f32),
            pltpu.VMEM((tokens, HSZ), f32),
            pltpu.VMEM((tokens, HSZ), bf),
            pltpu.VMEM((tokens, HSZ), bf),
            wide,
            wide,
            wide,
            wide,
            wide,
            pltpu.VMEM((3, rows, model // heads), bf),
            pltpu.VMEM((3, rows, model // heads), bf),
            pltpu.VMEM((groups, rows, tokens), f32),
            dma((6,)),
        ]
        + sems,
        compiler_params=pltpu.CompilerParams(
            collective_id=0, has_side_effects=True, vmem_limit_bytes=58 * 2**20
        ),
    )(queries, keys, values, bucket.reshape(1, -1), w_out, grad_out)
    return pl.pallas_call(
        place_kernel,
        out_shape=tuple(jax.ShapeDtypeStruct(shape, dtype) for shape, dtype in shapes),
        in_specs=[vmem] * 5,
        out_specs=(hbm,) * 5,
        scratch_shapes=[dma((5,))],
    )(*[pltpu.with_memory_space_constraint(one, pltpu.VMEM) for one in made])


def choose(queries, keys, values, bucket, w_out, grad_out):
    groups = queries.shape[1] // HSZ
    dense = groups == 4 and lax.axis_size("seq") == 8 and lax.axis_size("head") == 4
    plan = dense_device if dense else per_device
    return plan(queries, keys, values, bucket, w_out, grad_out)


def solution(mesh):
    return jax.shard_map(
        choose,
        mesh=mesh,
        in_specs=(
            P("seq", "head"),
            P("seq", "head"),
            P("seq", "head"),
            P(),
            P("head", None),
            P("seq", None),
        ),
        out_specs=(
            P("seq", "head"),
            P("seq", "head"),
            P("seq", "head"),
            P("seq", "head"),
            P("head", "seq"),
        ),
        check_vma=False,
    )
```

```python
import functools
import math

import jax
import jax.numpy as jnp
from jax import lax
from jax.experimental import pallas as pl
from jax.experimental.pallas import tpu as pltpu
from jax.sharding import PartitionSpec as P

HSZ = 128


def passed_along(value, axis, by):
    length = lax.axis_size(axis)
    pairs = [(i, i + by) for i in range(length) if 0 <= i + by < length]
    return lax.ppermute(value, axis, pairs)


def earlier_count(flags, axis):
    length = flags.shape[axis]
    at = jnp.arange(length)
    if axis == 0:
        before = (at[None, :] < at[:, None]).astype(jnp.float32)
        return jnp.dot(before, flags.astype(jnp.float32)).astype(jnp.int32)
    before = (at[:, None] < at[None, :]).astype(jnp.float32)
    return jnp.dot(flags.astype(jnp.float32), before).astype(jnp.int32)


def member_table(bucket_grid, owner, slot_count):
    matches = (bucket_grid == owner).astype(jnp.int32)
    ranking = earlier_count(matches, 1)
    slot_ids = jnp.arange(slot_count, dtype=jnp.int32)
    placed = matches[:, :, None] * (ranking[:, :, None] == slot_ids[None, None, :]).astype(
        jnp.int32
    )
    sources = bucket_grid.shape[0]
    stride = bucket_grid.shape[1]
    offsets = (
        jnp.arange(sources, dtype=jnp.int32)[:, None] * stride
        + jnp.arange(stride, dtype=jnp.int32)[None, :]
    )
    where_at = jnp.sum(placed * offsets[:, :, None], axis=1).reshape(-1)
    present = jnp.sum(placed, axis=1).reshape(-1)
    return (where_at, present)


def allowed_mask(where_here, alive_here, where_before, alive_before):
    amount = where_here.shape[0]
    asking = alive_here[:, None] > 0
    inside = (where_here[None, :] <= where_here[:, None]) & (alive_here[None, :] > 0) & asking
    inside = inside | (jnp.arange(amount)[:, None] == jnp.arange(amount)[None, :])
    earlier = (where_before[None, :] <= where_here[:, None]) & (alive_before[None, :] > 0) & asking
    return jnp.concatenate([inside, earlier], axis=1)


def softmax_rows(scores, allowed):
    masked = jnp.where(allowed[None], scores, -1e30)
    largest = jnp.max(masked, axis=2, keepdims=True)
    weights = jnp.where(allowed[None], jnp.exp(masked - largest), 0.0)
    return weights / jnp.sum(weights, axis=2, keepdims=True)


def local_slots(bucket_grid, device, sources, slot_total):
    my_buckets = lax.dynamic_index_in_dim(bucket_grid, device, 0, keepdims=False)
    owners = jnp.arange(sources, dtype=jnp.int32)
    onehot = (my_buckets[:, None] == owners[None, :]).astype(jnp.int32)
    ranking = jnp.sum(earlier_count(onehot, 0) * onehot, axis=1)
    back_index = my_buckets * slot_total + ranking
    slot_ids = jnp.arange(slot_total, dtype=jnp.int32)
    placed = onehot[:, :, None] * (ranking[:, None, None] == slot_ids[None, None, :]).astype(
        jnp.int32
    )
    token_ids = jnp.arange(my_buckets.shape[0], dtype=jnp.int32)
    send_index = jnp.sum(placed * token_ids[:, None, None], axis=0).reshape(-1)
    send_live = jnp.sum(placed, axis=0).reshape(-1)
    return (back_index, send_index, send_live)


def owner_probs(query_rows, key_all, allowed, scaling):
    scores = (
        jnp.einsum("qgd,kgd->gqk", query_rows, key_all, preferred_element_type=jnp.float32)
        * scaling
    )
    return softmax_rows(scores, allowed)


def owner_forward(probs, value_all):
    rounded = probs.astype(jnp.bfloat16)
    attended = jnp.einsum(
        "gqk,kgd->qgd", rounded, value_all, preferred_element_type=jnp.float32
    ).astype(jnp.bfloat16)
    return (rounded, attended)


def owner_backward(probs, rounded, attended, grad_rows, query_rows, key_all, value_all, scaling):
    centre = jnp.sum(attended.astype(jnp.float32) * grad_rows.astype(jnp.float32), axis=2)
    dprobs = jnp.einsum("qgd,kgd->gqk", grad_rows, value_all, preferred_element_type=jnp.float32)
    dscores = probs * (dprobs - jnp.transpose(centre)[:, :, None])
    dround = dscores.astype(jnp.bfloat16)
    grad_query = (
        jnp.einsum("gqk,kgd->qgd", dround, key_all, preferred_element_type=jnp.float32) * scaling
    ).astype(jnp.bfloat16)
    grad_key = (
        jnp.einsum("gqk,qgd->kgd", dround, query_rows, preferred_element_type=jnp.float32) * scaling
    )
    grad_value = jnp.einsum("gqk,qgd->kgd", rounded, grad_rows, preferred_element_type=jnp.float32)
    return (grad_query, grad_key, grad_value)


def with_previous(key_rows, value_rows):
    key_before, value_before = passed_along((key_rows, value_rows), "seq", 1)
    return (
        jnp.concatenate([key_rows, key_before], axis=0),
        jnp.concatenate([value_rows, value_before], axis=0),
    )


def settle_keys(grad_key, grad_value, slot_rows):
    key_next, value_next = passed_along(
        (grad_key[slot_rows:].astype(jnp.bfloat16), grad_value[slot_rows:].astype(jnp.bfloat16)),
        "seq",
        -1,
    )
    key_total = (grad_key[:slot_rows] + key_next.astype(jnp.float32)).astype(jnp.bfloat16)
    value_total = (grad_value[:slot_rows] + value_next.astype(jnp.float32)).astype(jnp.bfloat16)
    return (key_total, value_total)


def per_device(queries, keys, values, bucket, w_out, grad_out):
    sources = lax.axis_size("seq")
    device = lax.axis_index("seq")
    token_rows = queries.shape[0]
    features = queries.shape[1]
    groups = features // HSZ
    slot_total = max(2, 3 * token_rows // (2 * sources))
    slot_rows = sources * slot_total
    scaling = 1.0 / math.sqrt(HSZ)
    bucket_grid = bucket[:, 0].reshape(sources, token_rows)
    back_index, send_index, send_live = local_slots(bucket_grid, device, sources, slot_total)
    where_here, alive_here = member_table(bucket_grid, device, slot_total)
    where_before, alive_before = member_table(bucket_grid, device - 1, slot_total)
    allowed = allowed_mask(where_here, alive_here, where_before, alive_before)
    grad_heads = lax.dot_general(
        grad_out, w_out, (((1,), (1,)), ((), ())), preferred_element_type=jnp.float32
    ).astype(jnp.bfloat16)

    def pack_rows(source):
        return jnp.take(source, send_index, axis=0) * send_live[:, None].astype(source.dtype)

    def split_heads(block):
        return block.reshape(block.shape[0], groups, HSZ)

    def flatten(block):
        return block.reshape(block.shape[0], features)

    query_rows, key_rows, value_rows = (
        lax.all_to_all(pack_rows(queries), "seq", split_axis=0, concat_axis=0, tiled=True),
        lax.all_to_all(pack_rows(keys), "seq", split_axis=0, concat_axis=0, tiled=True),
        lax.all_to_all(pack_rows(values), "seq", split_axis=0, concat_axis=0, tiled=True),
    )
    key_all, value_all = with_previous(key_rows, value_rows)
    probs = owner_probs(split_heads(query_rows), split_heads(key_all), allowed, scaling)
    rounded, attended = owner_forward(probs, split_heads(value_all))
    key_all, value_all, probs, rounded, attended = (key_all, value_all, probs, rounded, attended)
    returned = lax.all_to_all(flatten(attended), "seq", split_axis=0, concat_axis=0, tiled=True)
    grad_rows = lax.all_to_all(
        pack_rows(grad_heads), "seq", split_axis=0, concat_axis=0, tiled=True
    )
    grad_query, grad_key, grad_value = owner_backward(
        probs,
        rounded,
        attended,
        split_heads(grad_rows),
        split_heads(query_rows),
        split_heads(key_all),
        split_heads(value_all),
        scaling,
    )
    key_total, value_total = settle_keys(flatten(grad_key), flatten(grad_value), slot_rows)
    back_query, back_key, back_value = (
        lax.all_to_all(flatten(grad_query), "seq", split_axis=0, concat_axis=0, tiled=True),
        lax.all_to_all(key_total, "seq", split_axis=0, concat_axis=0, tiled=True),
        lax.all_to_all(value_total, "seq", split_axis=0, concat_axis=0, tiled=True),
    )
    attended_home = jnp.take(returned, back_index, axis=0)
    partial_value = jnp.dot(attended_home, w_out, preferred_element_type=jnp.float32)
    layer_out = lax.psum_scatter(
        partial_value.astype(jnp.bfloat16), "head", scatter_dimension=1, tiled=True
    )
    weight_terms = lax.dot_general(
        attended_home, grad_out, (((0,), (0,)), ((), ())), preferred_element_type=jnp.float32
    )
    grad_weight = lax.psum_scatter(weight_terms, "seq", scatter_dimension=1, tiled=True)
    grad_queries = jnp.take(back_query, back_index, axis=0)
    grad_keys = jnp.take(back_key, back_index, axis=0)
    grad_values = jnp.take(back_value, back_index, axis=0)
    return (layer_out, grad_queries, grad_keys, grad_values, grad_weight)


MESH = pl.DeviceIdType.MESH
NT = (((1,), (1,)), ((), ()))
TN = (((0,), (0,)), ((), ()))


def times(a, b, dims):
    return lax.dot_general(a, b, dims, preferred_element_type=jnp.float32)


def dense_kernel(
    seqs,
    heads,
    q_hbm,
    k_hbm,
    v_hbm,
    brow,
    w_hbm,
    go_hbm,
    lo_out,
    gq_out,
    gk_out,
    gv_out,
    gw_out,
    w_buf,
    go_buf,
    gh_buf,
    q_buf,
    g_buf,
    k_buf,
    v_buf,
    go_all,
    att_all,
    dq_send,
    dk_acc,
    dv_acc,
    dk_send,
    dv_send,
    dq_in,
    dk_in,
    dv_in,
    dk_far,
    dv_far,
    lo_send,
    lo_in,
    p_buf,
    local_sem,
    in_send,
    in_recv,
    far_send,
    far_recv,
    go_send,
    go_recv,
    gx_send,
    gx_recv,
    att_send,
    att_recv,
    fwd_send,
    fwd_recv,
    dq_ssem,
    dq_rsem,
    dk_ssem,
    dk_rsem,
    dkf_ssem,
    dkf_rsem,
    lo_ssem,
    lo_rsem,
):
    s = lax.axis_index("seq")
    h = lax.axis_index("head")
    rows = q_hbm.shape[0]
    width = HSZ
    groups = q_hbm.shape[1] // width
    half = lax.div(s, groups)
    mine = lax.rem(s, groups)
    part = groups * rows
    scaling = 1.0 / math.sqrt(HSZ)
    gcols = w_hbm.shape[1] // seqs
    lcols = w_hbm.shape[1] // heads
    quarter = rows // heads
    low = half == 0
    high = half == 1
    deep = lax.div(mine, 2)

    def flip(index, bits):
        out = index
        for bit in (1, 2, 4):
            if bits & bit:
                out = out + bit * (1 - 2 * lax.rem(lax.div(index, bit), 2))
        return out

    def near(r):
        return flip(mine, r)

    def rows_of(block):
        return pl.ds(pl.multiple_of(block * rows, rows), rows)

    def cols_of(block, size=width):
        return pl.ds(pl.multiple_of(block * size, size), size)

    def quarter_of(head):
        return pl.ds(pl.multiple_of(head * quarter, quarter), quarter)

    def remote(src, dst, ssem, rsem, where):
        return pltpu.make_async_remote_copy(
            src_ref=src, dst_ref=dst, send_sem=ssem, recv_sem=rsem, device_id=where,
            device_id_type=MESH,
        )

    x_to, z_to, d_to = (flip(s, 1), h), (flip(s, 2), h), (flip(s, 3), h)
    c_to, across_to = (flip(s, 4), h), (s + 2 - 4 * half, h)
    core_to, y_to = (s, flip(h, 1)), (s, flip(h, 2))

    w_copy = pltpu.make_async_copy(w_hbm, w_buf, local_sem.at[0])
    go_copy = pltpu.make_async_copy(go_hbm, go_buf, local_sem.at[1])
    go_copy.start()
    w_copy.start()
    own = [
        pltpu.make_async_copy(k_hbm.at[:, cols_of(mine)], k_buf.at[rows_of(s), :], local_sem.at[2]),
        pltpu.make_async_copy(v_hbm.at[:, cols_of(mine)], v_buf.at[rows_of(s), :], local_sem.at[3]),
        pltpu.make_async_copy(q_hbm.at[:, cols_of(mine)], q_buf.at[rows_of(mine), :], local_sem.at[4]),
    ]
    for copy in own:
        copy.start()
    go_own = pltpu.make_async_copy(
        go_hbm.at[quarter_of(h), cols_of(s, gcols)], go_all.at[s, quarter_of(h), :], local_sem.at[5]
    )
    go_own.start()

    barrier = pltpu.get_barrier_semaphore()
    for r in range(1, seqs):
        pl.semaphore_signal(
            barrier, inc=1, device_id=(lax.rem(s + r, seqs), h), device_id_type=MESH
        )
    for there in (core_to, y_to):
        pl.semaphore_signal(barrier, inc=1, device_id=there, device_id_type=MESH)
    pl.semaphore_wait(barrier, seqs + 1)

    def cross_copies(sources, there_in, ssem, rsem):
        out = []
        for block in range(2):
            for side in range(2):
                to = 2 * block + lax.rem(mine + side, 2)
                for n, (src, dst) in enumerate(sources):
                    out.append(
                        remote(
                            src(to), dst, ssem.at[2 * block + side, n],
                            rsem.at[2 * deep + side, n], ((1 - half) * groups + to, there_in),
                        )
                    )
        return out

    def cross_arrivals(sources, ssem, rsem):
        return [
            remote(src(mine), dst, ssem.at[r, n], rsem.at[r, n], c_to)
            for r in range(groups)
            for n, (src, dst) in enumerate(sources)
        ]

    far_sources = (
        (lambda to: k_hbm.at[:, cols_of(to)], k_buf.at[rows_of(s), :]),
        (lambda to: v_hbm.at[:, cols_of(to)], v_buf.at[rows_of(s), :]),
    )
    far = cross_copies(far_sources, h, far_send, far_recv)
    far_in = cross_arrivals(far_sources, far_send, far_recv)

    @pl.when(low)
    def _():
        for copy in far[:4]:
            copy.start()

    inside = []
    for n, (src, dst, at) in enumerate(
        ((k_hbm, k_buf, s), (q_hbm, q_buf, mine), (v_hbm, v_buf, s))
    ):
        for r in (3, 2, 1):
            to = near(r)
            copy = remote(
                src.at[:, cols_of(to)], dst.at[rows_of(at), :], in_send.at[r, n],
                in_recv.at[r, n], (half * groups + to, h),
            )
            copy.start()
            inside.append(copy)
    spread = []
    for r in range(1, seqs):
        to = lax.rem(s + r, seqs)
        spread.append(
            remote(
                go_hbm.at[quarter_of(h), cols_of(to, gcols)], go_all.at[s, quarter_of(h), :],
                go_send.at[r], go_recv.at[s], (to, h),
            )
        )
    spread_in = [
        remote(
            go_hbm.at[quarter_of(h), cols_of(s, gcols)], go_all.at[source, quarter_of(h), :],
            go_send.at[0], go_recv.at[source], x_to,
        )
        for source in range(seqs)
    ]

    @pl.when(low)
    def _():
        for copy in far[4:]:
            copy.start()

    @pl.when(high)
    def _():
        for copy in spread:
            copy.start()

    @pl.when(high)
    def _():
        dk_far[...] = jnp.zeros_like(dk_far)
        dv_far[...] = jnp.zeros_like(dv_far)

    go_copy.wait()
    w_copy.wait()
    depth = w_buf.shape[1] // seqs

    def heads_step(c, total):
        at = pl.ds(pl.multiple_of(c * depth, depth), depth)
        return total + times(go_buf[:, at], w_buf[:, at], NT)

    gh = lax.fori_loop(
        0, seqs, heads_step, jnp.zeros((rows, groups * width), jnp.float32)
    )
    gh_buf[...] = gh.astype(jnp.bfloat16)
    gh_near = []
    for r in (3, 2, 1):
        to = near(r)
        copy = remote(
            gh_buf.at[:, cols_of(to)], g_buf.at[rows_of(mine), :], in_send.at[r, 3],
            in_recv.at[r, 3], (half * groups + to, h),
        )
        copy.start()
        gh_near.append(copy)
    g_buf[rows_of(mine), :] = gh_buf[:, cols_of(mine)]

    @pl.when(low)
    def _():
        for copy in spread:
            copy.start()

    for copy in own:
        copy.wait()
    for copy in inside:
        copy.wait_recv()

    @pl.when(high)
    def _():
        for copy in far_in:
            copy.wait_recv()

    def piece(token, head, kind, there):
        at = att_all.at[rows_of(token), cols_of(head)]
        lane, step = kind
        return remote(at, at, att_send.at[lane, step], att_recv.at[lane, step], there)

    def onward(token, head, out, into, step, there):
        at = att_all.at[rows_of(token), cols_of(head)]
        return remote(at, at, fwd_send.at[out, step], fwd_recv.at[into, step], there)

    def own_token(bits):
        return half * groups + near(bits)

    def other_token(bits):
        return (1 - half) * groups + near(bits)

    diagonal = lax.broadcasted_iota(jnp.int32, (rows, rows), 0) == lax.broadcasted_iota(
        jnp.int32, (rows, rows), 1
    )
    order = (3, 2, 1, 0)
    def go_part(first, head, index, where):
        at = go_all.at[pl.ds(first, groups), quarter_of(head), :]
        return remote(at, at, gx_send.at[index], gx_recv.at[index], where)

    go_moves = [
        [
            go_part(first, h, 3 * n, y_to),
            go_part(first, h, 3 * n + 1, core_to),
            go_part(first, flip(h, 2), 3 * n + 2, core_to),
        ]
        for n, first in enumerate((groups, 0))
    ]

    def go_exchange(n):
        first = (groups, 0)[n]

        @pl.when(half == 1 - n)
        def _():
            go_own.wait()

        for source in range(first, first + groups):

            @pl.when(s != source)
            def _():
                spread_in[source].wait_recv()

        go_moves[n][0].start()
        go_moves[n][1].start()

    att_x, att_z, att_c, att_h, att_d = {}, {}, {}, {}, {}
    dq_near = []
    def forward(step, block, token, span):
        qc = q_buf[rows_of(block), :]
        k_all = k_buf[:span, :]
        v_all = v_buf[:span, :]
        along = brow[:, cols_of(token, rows)].astype(jnp.float32)
        gap = jnp.sum(jnp.where(diagonal, along, 0.0), axis=1, keepdims=True)
        gap = gap - brow[:, :span].astype(jnp.float32)
        keys_at = lax.broadcasted_iota(jnp.int32, (rows, span), 1)
        query_at = token * rows + lax.broadcasted_iota(jnp.int32, (rows, span), 0)
        allowed = ((gap == 0.0) | (gap == 1.0)) & (keys_at <= query_at)
        scores = jnp.where(allowed, times(qc, k_all, NT) * scaling, -1e30)
        largest = jnp.max(scores, axis=1, keepdims=True)
        weights = jnp.where(allowed, jnp.exp(scores - largest), 0.0)
        probs = weights * (1.0 / jnp.sum(weights, axis=1, keepdims=True))
        p_buf[step, :, :span] = probs
        att_all[rows_of(token), cols_of(mine)] = jnp.dot(
            probs.astype(jnp.bfloat16), v_all, preferred_element_type=jnp.float32
        ).astype(jnp.bfloat16)

    def backward(step, block, token, span, dq_to):
        qc = q_buf[rows_of(block), :]
        gc = g_buf[rows_of(block), :]
        k_all = k_buf[:span, :]
        probs = p_buf[step, :, :span]
        attended = att_all[rows_of(token), cols_of(mine)]
        centre = jnp.sum(
            attended.astype(jnp.float32) * gc.astype(jnp.float32), axis=1, keepdims=True
        )
        dscores = (probs * (times(gc, v_buf[:span, :], NT) - centre)).astype(jnp.bfloat16)
        dq_to[...] = (
            jnp.dot(dscores, k_all, preferred_element_type=jnp.float32) * scaling
        ).astype(jnp.bfloat16)
        dk = times(dscores, qc, TN)
        dv = times(probs.astype(jnp.bfloat16), gc, TN)
        if step == 0:
            dk_acc[:span, :] = dk
            dv_acc[:span, :] = dv
        else:
            dk_acc[:span, :] += dk
            dv_acc[:span, :] += dv

    def by_half(work, *args):
        @pl.when(low)
        def _():
            work(part, *args)

        @pl.when(high)
        def _():
            work(2 * part, *args)

    for step, r in enumerate(order):
        block = near(r)
        token = half * groups + block
        by_half(lambda span, step=step, block=block, token=token: forward(step, block, token, span))
        if r == 3:
            att_d[r] = piece(token, mine, (3, step), d_to)
            att_d[r].start()
        att_c[r] = onward(token, mine, 1, 1, step, across_to)
        att_h[r] = onward(token, mine, 1, 0, step, c_to)
        att_z[r] = piece(token, mine, (1, step), z_to)
        att_x[r] = piece(token, mine, (0, step), x_to)
        for copy in (att_z[r], att_x[r]):
            copy.start()

        @pl.when(deep - half == 1)
        def _():
            att_c[r].start()

        @pl.when(high)
        def _():
            att_h[r].start()


    kept, mate = {}, {}
    kept_z, mate_z, kept_x, mate_x = {}, {}, {}, {}
    for step, r in enumerate(order):
        kept[r] = onward(other_token(r), mine, 0, 0, step, z_to)
        mate[r] = onward(other_token(2 ^ r), near(2), 1, 1, step, z_to)
        kept_z[r] = onward(other_token(r), mine, 2, 1, step, z_to)
        mate_z[r] = onward(other_token(2 ^ r), near(2), 3, 0, step, z_to)
        kept_x[r] = onward(other_token(r), mine, 4, 2, step, x_to)
        mate_x[r] = onward(other_token(2 ^ r), near(2), 5, 3, step, x_to)

    def pass_kept():
        for r in order:
            kept[r].wait_recv()
            kept_x[r].start()

            @pl.when(half + deep < 2)
            def _():
                kept_z[r].start()

    def pass_mate():
        for r in order:
            mate[r].wait_recv()
            mate_x[r].start()

            @pl.when(half - deep == 1)
            def _():
                mate_z[r].start()

    def pass_first():
        @pl.when(half - deep == 1)
        def _():
            pass_mate()

        @pl.when(half - deep != 1)
        def _():
            pass_kept()

    def pass_second():
        @pl.when(half - deep == 1)
        def _():
            pass_kept()

        @pl.when(half - deep != 1)
        def _():
            pass_mate()

    go_exchange(0)

    @pl.when(low)
    def _():
        go_exchange(1)

    for copy in gh_near:
        copy.wait_recv()
    for step, r in enumerate(order):
        block = near(r)
        token = half * groups + block
        dq_to = dq_in.at[:, cols_of(mine)] if r == 0 else dq_send.at[r]
        by_half(
            lambda span, step=step, block=block, token=token, dq_to=dq_to: backward(
                step, block, token, span, dq_to
            )
        )
        if r != 0:
            copy = remote(
                dq_send.at[r], dq_in.at[:, cols_of(mine)], dq_ssem.at[r], dq_rsem.at[r],
                (token, h),
            )
            copy.start()
            dq_near.append(copy)

    def round_terms(span):
        dk_send[:span, :] = (dk_acc[:span, :] * scaling).astype(jnp.bfloat16)
        dv_send[:span, :] = dv_acc[:span, :].astype(jnp.bfloat16)

    by_half(round_terms)
    dk_sources = (
        (lambda to: dk_send.at[rows_of(to), :], dk_far.at[:, cols_of(mine)]),
        (lambda to: dv_send.at[rows_of(to), :], dv_far.at[:, cols_of(mine)]),
    )
    dk_cross = cross_copies(dk_sources, h, dkf_ssem, dkf_rsem)
    dk_cross_in = cross_arrivals(dk_sources, dkf_ssem, dkf_rsem)


    dk_near = []
    for r in range(1, groups):
        to = near(r)
        for n, (src, dst) in enumerate(((dk_send, dk_in), (dv_send, dv_in))):
            copy = remote(
                src.at[rows_of(half * groups + to), :], dst.at[:, cols_of(mine)],
                dk_ssem.at[r, n], dk_rsem.at[r, n], (half * groups + to, h),
            )
            copy.start()
            dk_near.append(copy)
    @pl.when(high)
    def _():
        for copy in dk_cross:
            copy.start()

    dk_in[:, cols_of(mine)] = dk_send[rows_of(s), :]
    dv_in[:, cols_of(mine)] = dv_send[rows_of(s), :]


    @pl.when(high)
    def _():
        go_exchange(1)

    fwd_near, fwd_across = {}, {}
    for step, r in enumerate(order):
        fwd_near[r] = onward(own_token(2 ^ r), near(2), 6, 4, step, x_to)
        fwd_across[r] = onward(own_token(2 ^ r), near(2), 0, 0, step, across_to)
        att_z[r].wait_recv()
        if r != 3:
            fwd_near[r].start()

        @pl.when(deep - half == 1)
        def _():
            fwd_across[r].start()


    @pl.when(half - deep == 1)
    def _():
        pass_first()

    go_moves[0][0].wait_recv()
    go_moves[0][2].start()

    @pl.when(low)
    def _():
        go_moves[1][0].wait_recv()
        go_moves[1][2].start()


    att_x[1].wait_recv()
    att_d[3].wait_recv()
    home = att_all[rows_of(s), :]

    def partial_for(head):
        return jnp.dot(home, w_buf[:, cols_of(head, lcols)], preferred_element_type=jnp.float32)

    lo_moves = [
        remote(lo_send.at[0], lo_in.at[0], lo_ssem.at[0], lo_rsem.at[0], core_to),
        remote(lo_send.at[1], lo_in.at[1], lo_ssem.at[1], lo_rsem.at[1], core_to),
        remote(lo_send.at[2], lo_in.at[2], lo_ssem.at[2], lo_rsem.at[2], y_to),
    ]
    lo_send[0] = partial_for(flip(h, 3)).astype(jnp.bfloat16)
    lo_moves[0].start()
    across = partial_for(flip(h, 2))
    lo_moves[0].wait_recv()
    lo_send[2] = (across + lo_in[0].astype(jnp.float32)).astype(jnp.bfloat16)
    lo_moves[2].start()
    lo_send[1] = partial_for(flip(h, 1)).astype(jnp.bfloat16)
    lo_moves[1].start()
    layer = partial_for(h)


    @pl.when(half - deep == 1)
    def _():
        pass_second()


    @pl.when(half + deep == 2)
    def _():
        pass_first()


    @pl.when(half + deep == 2)
    def _():
        pass_second()


    @pl.when(low)
    def _():
        pass_first()


    @pl.when(low)
    def _():
        pass_second()

    def weight_rows(bits):
        head = near(bits)
        gw_out[rows_of(head), :] = times(
            att_all[:, cols_of(head)], go_all[...].reshape(seqs * rows, gcols), TN
        )


    @pl.when(high)
    def _():
        go_moves[1][0].wait_recv()
        go_moves[1][2].start()

    for n in range(2):
        go_moves[n][1].wait_recv()
        go_moves[n][2].wait_recv()
    weight_rows(0)
    weight_rows(2)
    for copy in dq_near:
        copy.wait_recv()
    gq_out[...] = dq_in[...]
    lo_moves[1].wait_recv()
    lo_moves[2].wait_recv()
    lo_out[...] = (layer + lo_in[1].astype(jnp.float32) + lo_in[2].astype(jnp.float32)).astype(
        jnp.bfloat16
    )
    for r in order:
        if r != 1:
            att_x[r].wait_recv()
        kept_x[r].wait_recv()
    weight_rows(1)
    for r in order:
        if r != 3:
            fwd_near[r].wait_recv()
        mate_x[r].wait_recv()
    weight_rows(3)
    for copy in dk_near:
        copy.wait_recv()

    @pl.when(low)
    def _():
        for copy in dk_cross_in:
            copy.wait_recv()

    gk_out[...] = (dk_in[...].astype(jnp.float32) + dk_far[...].astype(jnp.float32)).astype(
        jnp.bfloat16
    )
    gv_out[...] = (dv_in[...].astype(jnp.float32) + dv_far[...].astype(jnp.float32)).astype(
        jnp.bfloat16
    )

    moved = inside + gh_near + spread + go_moves[0] + go_moves[1] + dq_near + dk_near + lo_moves
    del fwd_near[3]
    for group in (att_x, att_z, att_d, fwd_near, kept_x, mate_x):
        moved += list(group.values())
    for copy in moved:
        copy.wait_send()

    @pl.when(deep - half == 1)
    def _():
        for group in (att_c, fwd_across):
            for copy in group.values():
                copy.wait_send()

    @pl.when(high)
    def _():
        for copy in att_h.values():
            copy.wait_send()

    @pl.when(half + deep < 2)
    def _():
        for copy in kept_z.values():
            copy.wait_send()

    @pl.when(half - deep == 1)
    def _():
        for copy in mate_z.values():
            copy.wait_send()

    @pl.when(low)
    def _():
        for copy in far:
            copy.wait_send()

    @pl.when(high)
    def _():
        for copy in dk_cross:
            copy.wait_send()


def place_kernel(*refs):
    sem = refs[-1]
    half = len(refs) // 2
    copies = [
        pltpu.make_async_copy(refs[n], refs[half + n], sem.at[n]) for n in range(half)
    ]
    for copy in copies:
        copy.start()
    for copy in copies:
        copy.wait()


def dense_device(queries, keys, values, bucket, w_out, grad_out):
    seqs = lax.axis_size("seq")
    heads = lax.axis_size("head")
    rows, features = queries.shape
    model = w_out.shape[1]
    groups = features // HSZ
    part = groups * rows
    tokens = seqs * rows
    bf, f32 = jnp.bfloat16, jnp.float32
    vmem = pl.BlockSpec(memory_space=pltpu.VMEM)
    hbm = pl.BlockSpec(memory_space=pl.ANY)
    dma = pltpu.SemaphoreType.DMA
    wide = pltpu.VMEM((rows, features), bf)
    sems = []
    for shape in (
        (groups, 4), (groups, 2), (seqs,), (6,), (4, groups), (7, groups), (groups,), (groups, 2),
        (groups, 2), (3,),
    ):
        sems += [dma(shape), dma(shape)]
    shapes = (
        ((rows, model // heads), bf),
        ((rows, features), bf),
        ((rows, features), bf),
        ((rows, features), bf),
        ((features, model // seqs), f32),
    )
    made = pl.pallas_call(
        functools.partial(dense_kernel, seqs, heads),
        out_shape=tuple(pltpu.VMEM(shape, dtype) for shape, dtype in shapes),
        in_specs=[hbm, hbm, hbm, vmem, hbm, hbm],
        out_specs=(vmem,) * 5,
        scratch_shapes=[
            pltpu.VMEM(w_out.shape, bf),
            pltpu.VMEM(grad_out.shape, bf),
            wide,
            pltpu.VMEM((part, HSZ), bf),
            pltpu.VMEM((part, HSZ), bf),
            pltpu.VMEM((tokens, HSZ), bf),
            pltpu.VMEM((tokens, HSZ), bf),
            pltpu.VMEM((seqs, rows, model // seqs), bf),
            pltpu.VMEM((tokens, features), bf),
            pltpu.VMEM((groups, rows, HSZ), bf),
            pltpu.VMEM((tokens, HSZ), f32),
            pltpu.VMEM((tokens, HSZ), f32),
            pltpu.VMEM((tokens, HSZ), bf),
            pltpu.VMEM((tokens, HSZ), bf),
            wide,
            wide,
            wide,
            wide,
            wide,
            pltpu.VMEM((3, rows, model // heads), bf),
            pltpu.VMEM((3, rows, model // heads), bf),
            pltpu.VMEM((groups, rows, tokens), f32),
            dma((6,)),
        ]
        + sems,
        compiler_params=pltpu.CompilerParams(
            collective_id=0, has_side_effects=True, vmem_limit_bytes=58 * 2**20
        ),
    )(queries, keys, values, bucket.reshape(1, -1), w_out, grad_out)
    return pl.pallas_call(
        place_kernel,
        out_shape=tuple(jax.ShapeDtypeStruct(shape, dtype) for shape, dtype in shapes),
        in_specs=[vmem] * 5,
        out_specs=(hbm,) * 5,
        scratch_shapes=[dma((5,))],
    )(*[pltpu.with_memory_space_constraint(one, pltpu.VMEM) for one in made])


def choose(queries, keys, values, bucket, w_out, grad_out):
    groups = queries.shape[1] // HSZ
    dense = groups == 4 and lax.axis_size("seq") == 8 and lax.axis_size("head") == 4
    plan = dense_device if dense else per_device
    return plan(queries, keys, values, bucket, w_out, grad_out)


def solution(mesh):
    return jax.shard_map(
        choose,
        mesh=mesh,
        in_specs=(
            P("seq", "head"),
            P("seq", "head"),
            P("seq", "head"),
            P(),
            P("head", None),
            P("seq", None),
        ),
        out_specs=(
            P("seq", "head"),
            P("seq", "head"),
            P("seq", "head"),
            P("seq", "head"),
            P("head", "seq"),
        ),
        check_vma=False,
    )
```
